512 devices in a mesh: row: 32 (over x_lo, y, core), col: 16 (over x_hi, z).
Axes of the slice: x: 4 (x_hi: 2, x_lo: 2; x = x_hi * 2 + x_lo), y: 8, z: 8, core: 2. Of those that a mesh axis runs over, the one named last changes fastest.
Arguments:
- front_init: float32 [16, 16, 2, 4096], P(None, None, None, 'row'), may hold values from -3 to 3
- green_hist: float32 [256, 16, 2, 4096], P('row', None, None, 'col'), may hold values from -0.0625 to 0.0625
- field_hist: float32 [256, 16, 2, 4096], P('row', None, None, 'col'), may hold values from -0.0625 to 0.0625
Outputs:
- front_final: float32 [16, 16, 2, 4096], P(None, None, None, 'row')
The draws below stay inside these ranges and needn't reach their ends.
All inputs are finite; a program needn't handle non-finite values.
Results may differ from the reference program's by a relative error of at most 0.0001.
Values sent between devices are 32-bit elements; how exact they have to be, the bound alone decides.
No kernel may reach another device: no remote copies, remote signals or barrier semaphores. Data moves between devices by JAX's collectives and lax.ppermute only.
A program may use at most 64 MiB of HBM per device.

```python
import jax
import jax.numpy as jnp
from jax import lax

NO = 16
FR = 16
ITERS = 2
NT = 256


def block_scale(rng, shape, cuts, least, top_value):
    def one(axis_at, shards_of):
        heights = jax.random.uniform(jax.random.fold_in(jax.random.fold_in(rng, 6), axis_at), (shards_of,), jnp.float32, least / len(cuts), top_value / len(cuts))
        return jnp.repeat(jnp.exp(heights), shape[axis_at] // shards_of).reshape((-1,) + (1,) * (len(shape) - axis_at - 1))

    level = one(*cuts[0])
    for cut in cuts[1:]:
        level = level * one(*cut)
    return level


def bell_draw(own_key, shape, width, most, cuts=(), held_as=jnp.bfloat16):
    drawn = width * jax.random.normal(own_key, shape, jnp.float32)
    if cuts:
        drawn = drawn * block_scale(own_key, shape, cuts, -0.22, 0.18)
    return jnp.clip(drawn, -most, most).astype(held_as)


def setup_inputs(seed: int = 0) -> dict:
    arg_keys = jax.random.split(jax.random.key(seed), 4)
    front_init = bell_draw(arg_keys[0], (FR, NO, 2, NT * NO), 0.5, 3.0, ((3, 32),), jnp.float32)
    green_hist = bell_draw(arg_keys[1], (NT, NO, 2, NT * NO), (2 * NT * NO) ** -0.5, 0.0625, ((0, 32), (3, 16)), jnp.float32)
    field_hist = bell_draw(arg_keys[2], (NT, NO, 2, NT * NO), (2 * NT * NO) ** -0.5, 0.0625, ((0, 32), (3, 16)), jnp.float32)
    return dict(front_init=front_init, green_hist=green_hist, field_hist=field_hist)


STEP_WEIGHT = 0.5


def product(left, right):
    return jnp.dot(left, right, precision=lax.Precision.HIGHEST, preferred_element_type=jnp.float32)


def cubic_sigma(current):
    count, orbits, parts, length = current.shape
    swapped = current.reshape(count, orbits, parts, length // orbits, orbits)
    swapped = swapped.transpose(0, 4, 2, 3, 1).reshape(current.shape)
    real_part = current[:, :, 0, :]
    imag_part = current[:, :, 1, :]
    square_re = real_part * real_part - imag_part * imag_part
    square_im = 2.0 * real_part * imag_part
    other_re = swapped[:, :, 0, :]
    other_im = swapped[:, :, 1, :]
    sigma_re = square_re * other_re + square_im * other_im
    sigma_im = square_im * other_re - square_re * other_im
    return sigma_re, sigma_im


def collide(current, green_re, green_im, field_re, field_im):
    count, orbits, parts, length = current.shape
    sigma_re, sigma_im = cubic_sigma(current)
    sigma_re = sigma_re.reshape(count * orbits, length)
    sigma_im = sigma_im.reshape(count * orbits, length)
    front_re = current[:, :, 0, :].reshape(count * orbits, length)
    front_im = current[:, :, 1, :].reshape(count * orbits, length)
    image_re = product(sigma_re, green_re) - product(sigma_im, green_im) + product(front_re, field_re) - product(front_im, field_im)
    image_im = product(sigma_re, green_im) + product(sigma_im, green_re) + product(front_re, field_im) + product(front_im, field_re)
    image_re = image_re.reshape(count, orbits, -1)
    image_im = image_im.reshape(count, orbits, -1)
    return jnp.stack([image_re, image_im], axis=2)


def matrices(history):
    rows = history.shape[0] * history.shape[1]
    return history[:, :, 0, :].reshape(rows, -1), history[:, :, 1, :].reshape(rows, -1)


def reference(front_init, green_hist, field_hist):
    green_re, green_im = matrices(green_hist)
    field_re, field_im = matrices(field_hist)
    current = front_init
    for sweep in range(ITERS):
        current = front_init + STEP_WEIGHT * collide(current, green_re, green_im, field_re, field_im)
    return current
```

```python
import functools

import jax
import jax.numpy as jnp
from jax import lax
from jax.experimental import pallas as pl
from jax.experimental.pallas import tpu as pltpu
from jax.sharding import Mesh, PartitionSpec as P

ITERS = 2
STEP_WEIGHT = 0.5

A = ("xl", "y")
B = ("xh", "z")
EVERY = ("xl", "y", "core", "xh", "z")


def split(value):
    high = value.astype(jnp.bfloat16)
    low = (value - high.astype(jnp.float32)).astype(jnp.bfloat16)
    return high, low


def dot3(left, right):
    def one(x, y):
        return jnp.dot(x, y, preferred_element_type=jnp.float32)
    return one(left[0], right[0]) + (one(left[0], right[1]) + one(left[1], right[0]))


def swap_orbitals(value, orbits):
    rows, lanes = value.shape
    row = lax.broadcasted_iota(jnp.int32, value.shape, 0)
    lane = lax.broadcasted_iota(jnp.int32, value.shape, 1)
    step = 1
    while step < orbits:
        row_bit = (row // step) % 2
        lane_bit = (lane // step) % 2
        up = pltpu.roll(pltpu.roll(value, step, 1), rows - step, 0)
        down = pltpu.roll(pltpu.roll(value, lanes - step, 1), step, 0)
        value = jnp.where(row_bit == lane_bit, value, jnp.where(row_bit == 0, up, down))
        step *= 2
    return value


def collide_kernel(orbits, order, updated, core_ref, init_ref, *refs):
    if updated:
        arrived_ref, green_ref, field_ref, own_ref, other_ref, cur_ref = refs
        cur_ref[...] = init_ref[...] + STEP_WEIGHT * arrived_ref[...]
        source = cur_ref
    else:
        green_ref, field_ref, own_ref, other_ref = refs
        source = init_ref
    pairs = source.shape[0] // 2
    re = source[pl.ds(0, pairs, stride=2), :]
    im = source[pl.ds(1, pairs, stride=2), :]
    other_re = swap_orbitals(re, orbits)
    other_im = swap_orbitals(im, orbits)
    square_re = re * re - im * im
    square_im = 2.0 * re * im
    sigma_re = square_re * other_re + square_im * other_im
    sigma_im = square_im * other_re - square_re * other_im
    left_re = split(jnp.concatenate([sigma_re, re], axis=1))
    left_im = split(jnp.concatenate([sigma_im, im], axis=1))
    depth = green_ref.shape[0] // 4
    first = core_ref[0] == 0

    def history(half, part):
        pick = pl.ds(2 * half + part, depth, stride=4)
        return jnp.concatenate([green_ref[pick, :], field_ref[pick, :]], axis=0)

    right_re = split(jnp.concatenate([history(0, 0), history(1, 0)], axis=1))
    right_im = split(jnp.concatenate([history(0, 1), history(1, 1)], axis=1))
    image_re = dot3(left_re, right_re) - dot3(left_im, right_im)
    image_im = dot3(left_re, right_im) + dot3(left_im, right_re)
    lanes = own_ref.shape[1]
    for part, image in ((0, image_re), (1, image_im)):
        low, high = image[:, :lanes], image[:, lanes:]
        own = jnp.where(first, low, high)
        other = jnp.where(first, high, low)
        for place, front in enumerate(order):
            here = pl.ds(place * 2 * orbits + part, orbits, stride=2)
            there = slice(front * orbits, (front + 1) * orbits)
            own_ref[here, :] = own[there]
            other_ref[here, :] = other[there]


def collide(core, init, arrived, green, field, orbits, order):
    block = jax.ShapeDtypeStruct(init.shape, jnp.float32)
    vmem = pl.BlockSpec(memory_space=pltpu.VMEM)
    operands = [init] + ([] if arrived is None else [arrived]) + [green, field]
    return pl.pallas_call(
        functools.partial(collide_kernel, orbits, order, arrived is not None),
        out_shape=(block, block),
        in_specs=[pl.BlockSpec(memory_space=pltpu.SMEM)] + [vmem] * len(operands),
        out_specs=(vmem, vmem),
        scratch_shapes=[] if arrived is None else [pltpu.VMEM(init.shape, jnp.float32)],
        name="collide",
    )(core, *operands)


def per_device(turn, ys, zs, front_init, green_hist, field_hist):
    fronts, orbits, parts, width = front_init.shape
    rows = fronts * orbits * parts
    init = front_init.reshape(rows, width)

    def tiles(history):
        times, inner, _, lanes = history.shape
        return history.reshape(times, inner, parts, lanes // width, width).transpose(
            0, 1, 3, 2, 4).reshape(-1, width)

    green, field = tiles(green_hist), tiles(field_hist)
    core = lax.axis_index("core").astype(jnp.int32).reshape(1)
    shift = zs // 2
    order = [x * ys + (y + shift) % ys for x in range(fronts // ys) for y in range(ys)]
    arrived = None
    for sweep in range(ITERS):
        own, other = collide(core, init, arrived, green, field, orbits, order)
        chip = own + lax.ppermute(other, "core", [(0, 1), (1, 0)])
        spread = lax.all_to_all(chip.reshape(fronts, -1, width), A, 0, 0, tiled=True)
        piece = jnp.sum(spread, axis=0)
        turned = lax.ppermute(piece, EVERY, turn)
        copies = jnp.broadcast_to(turned[None], (fronts,) + turned.shape)
        arrived = lax.all_to_all(copies, B, 0, 0, tiled=True).reshape(rows, width)
    return (init + STEP_WEIGHT * arrived).reshape(front_init.shape)


def solution(mesh):
    xls, ys, cores, xhs, zs = 2, 8, 2, 2, 8
    fine = Mesh(mesh.devices.reshape(xls, ys, cores, xhs, zs), EVERY)

    def place(xl, y, core, xh, z):
        return (((xl * ys + y) * cores + core) * xhs + xh) * zs + z

    turn = [
        (place(xl, y, core, xh, z), place(xh, z, core, xl, (y + zs // 2) % zs))
        for xl in range(xls) for y in range(ys) for core in range(cores)
        for xh in range(xhs) for z in range(zs)
    ]
    return jax.shard_map(
        functools.partial(per_device, turn, ys, zs),
        mesh=fine,
        in_specs=(
            P(None, None, None, ("xl", "y", "core")),
            P(("xl", "y", "core"), None, None, B),
            P(("xl", "y", "core"), None, None, B),
        ),
        out_specs=P(None, None, None, ("xl", "y", "core")),
        check_vma=False,
    )
```

```python
import functools

import jax
import jax.numpy as jnp
from jax import lax
from jax.experimental import pallas as pl
from jax.experimental.pallas import tpu as pltpu
from jax.sharding import Mesh, PartitionSpec as P


STEP_WEIGHT = 0.5

A = ("xl", "y")
B = ("xh", "z")
EVERY = ("xl", "y", "core", "xh", "z")


def split(value):
    high = value.astype(jnp.bfloat16)
    low = (value - high.astype(jnp.float32)).astype(jnp.bfloat16)
    return high, low


def dot3(left, right):
    def one(x, y):
        return jnp.dot(x, y, preferred_element_type=jnp.float32)

    return one(left[0], right[0]) + (one(left[0], right[1]) + one(left[1], right[0]))


def swap_orbitals(value, orbits):
    rows, lanes = value.shape
    row = lax.broadcasted_iota(jnp.int32, value.shape, 0)
    lane = lax.broadcasted_iota(jnp.int32, value.shape, 1)
    step = 1
    while step < orbits:
        row_bit = (row // step) % 2
        lane_bit = (lane // step) % 2
        up = pltpu.roll(pltpu.roll(value, step, 1), rows - step, 0)
        down = pltpu.roll(pltpu.roll(value, lanes - step, 1), step, 0)
        value = jnp.where(row_bit == lane_bit, value, jnp.where(row_bit == 0, up, down))
        step *= 2
    return value


def collide_kernel(orbits, order, updated, core_ref, init_ref, *refs):
    if updated:
        arrived_ref, green_ref, field_ref, own_ref, other_ref, cur_ref = refs
        cur_ref[...] = init_ref[...] + STEP_WEIGHT * arrived_ref[...]
        source = cur_ref
    else:
        green_ref, field_ref, own_ref, other_ref = refs
        source = init_ref
    pairs = source.shape[0] // 2
    re = source[pl.ds(0, pairs, stride=2), :]
    im = source[pl.ds(1, pairs, stride=2), :]
    other_re = swap_orbitals(re, orbits)
    other_im = swap_orbitals(im, orbits)
    square_re = re * re - im * im
    square_im = 2.0 * re * im
    sigma_re = square_re * other_re + square_im * other_im
    sigma_im = square_im * other_re - square_re * other_im
    left_re = split(jnp.concatenate([sigma_re, re], axis=1))
    left_im = split(jnp.concatenate([sigma_im, im], axis=1))
    depth = green_ref.shape[0] // 4
    first = core_ref[0] == 0

    def history(half, part):
        pick = pl.ds(2 * half + part, depth, stride=4)
        return jnp.concatenate([green_ref[pick, :], field_ref[pick, :]], axis=0)

    right_re = split(jnp.concatenate([history(0, 0), history(1, 0)], axis=1))
    right_im = split(jnp.concatenate([history(0, 1), history(1, 1)], axis=1))
    image_re = dot3(left_re, right_re) - dot3(left_im, right_im)
    image_im = dot3(left_re, right_im) + dot3(left_im, right_re)
    lanes = own_ref.shape[1]
    for part, image in ((0, image_re), (1, image_im)):
        low, high = image[:, :lanes], image[:, lanes:]
        own = jnp.where(first, low, high)
        other = jnp.where(first, high, low)
        for place, front in enumerate(order):
            here = pl.ds(place * 2 * orbits + part, orbits, stride=2)
            there = slice(front * orbits, (front + 1) * orbits)
            own_ref[here, :] = own[there]
            other_ref[here, :] = other[there]


def collide(core, init, arrived, green, field, orbits, order):
    block = jax.ShapeDtypeStruct(init.shape, jnp.float32)
    vmem = pl.BlockSpec(memory_space=pltpu.VMEM)
    operands = [init] + ([] if arrived is None else [arrived]) + [green, field]
    return pl.pallas_call(
        functools.partial(collide_kernel, orbits, order, arrived is not None),
        out_shape=(block, block),
        in_specs=[pl.BlockSpec(memory_space=pltpu.SMEM)] + [vmem] * len(operands),
        out_specs=(vmem, vmem),
        scratch_shapes=[] if arrived is None else [pltpu.VMEM(init.shape, jnp.float32)],
        compiler_params=pltpu.CompilerParams(vmem_limit_bytes=12 << 20),
        name="collide",
    )(core, *operands)


def per_device(flip, front_init, green_hist, field_hist):
    return corrector(flip, front_init, green_hist, field_hist)


def corrector(flip, front_init, green_hist, field_hist):
    fronts, orbits, parts, width = front_init.shape
    rows = fronts * orbits * parts
    init = front_init.reshape(rows, width)

    def tiles(history):
        times, inner, _, lanes = history.shape
        return history.reshape(times, inner, parts, lanes // width, width).transpose(
            0, 1, 3, 2, 4).reshape(-1, width)

    def place(axes):
        return lax.axis_index(axes[0]) * lax.axis_size(axes[1]) + lax.axis_index(axes[1])

    def piece_of(front, index):
        return lax.dynamic_slice_in_dim(front, index * (rows // fronts), rows // fronts, 0)

    green, field = tiles(green_hist), tiles(field_hist)
    core = lax.axis_index("core").astype(jnp.int32).reshape(1)
    order = list(range(fronts))
    green_flip = lax.ppermute(green, EVERY, flip)
    field_flip = lax.ppermute(field, EVERY, flip)
    own_piece = piece_of(init, place(B))
    flip_piece = lax.ppermute(own_piece, EVERY, flip)

    def sweep(current, green, field, start, axes):
        own, other = collide(core, current, None, green, field, orbits, order)
        chip = own + lax.ppermute(other, "core", [(0, 1), (1, 0)])
        spread = lax.all_to_all(chip.reshape(fronts, -1, width), axes, 0, 0, tiled=True)
        piece = start + STEP_WEIGHT * jnp.sum(spread, axis=0)
        copies = jnp.broadcast_to(piece[None], (fronts,) + piece.shape)
        return lax.all_to_all(copies, axes, 0, 0, tiled=True).reshape(rows, width)

    current = sweep(init, green, field, flip_piece, A)
    current = sweep(current, green_flip, field_flip, own_piece, B)
    return current.reshape(front_init.shape)


def solution(mesh):
    xls, ys, cores, xhs, zs = 2, 8, 2, 2, 8
    fine = Mesh(mesh.devices.reshape(xls, ys, cores, xhs, zs), EVERY)

    def place(xl, y, core, xh, z):
        return (((xl * ys + y) * cores + core) * xhs + xh) * zs + z

    flip = [
        (place(xl, y, core, xh, z), place(xh, z, core, xl, y))
        for xl in range(xls) for y in range(ys) for core in range(cores)
        for xh in range(xhs) for z in range(zs)
    ]
    return jax.shard_map(
        functools.partial(per_device, flip),
        mesh=fine,
        in_specs=(
            P(None, None, None, ("xl", "y", "core")),
            P(("xl", "y", "core"), None, None, B),
            P(("xl", "y", "core"), None, None, B),
        ),
        out_specs=P(None, None, None, ("xl", "y", "core")),
        check_vma=False,
    )
```

```python
import functools

import jax
import jax.numpy as jnp
from jax import lax
from jax.experimental import pallas as pl
from jax.experimental.pallas import tpu as pltpu
from jax.sharding import Mesh, PartitionSpec as P

ITERS = 2
STEP_WEIGHT = 0.5

A = ("xl", "y")
B = ("xh", "z")
EVERY = ("xl", "y", "core", "xh", "z")


def split(value):
    high = value.astype(jnp.bfloat16)
    low = (value - high.astype(jnp.float32)).astype(jnp.bfloat16)
    return high, low


def dot3(left, right):
    def one(x, y):
        return jnp.dot(x, y, preferred_element_type=jnp.float32)
    return one(left[0], right[0]) + (one(left[0], right[1]) + one(left[1], right[0]))


def swap_orbitals(value, orbits):
    rows, lanes = value.shape
    row = lax.broadcasted_iota(jnp.int32, value.shape, 0)
    lane = lax.broadcasted_iota(jnp.int32, value.shape, 1)
    step = 1
    while step < orbits:
        row_bit = (row // step) % 2
        lane_bit = (lane // step) % 2
        up = pltpu.roll(pltpu.roll(value, step, 1), rows - step, 0)
        down = pltpu.roll(pltpu.roll(value, lanes - step, 1), step, 0)
        value = jnp.where(row_bit == lane_bit, value, jnp.where(row_bit == 0, up, down))
        step *= 2
    return value


def collide_kernel(orbits, order, loads, core_ref, *refs):
    if loads:
        sources, (own_ref, other_ref), held, sems = refs[:3], refs[3:5], refs[5:8], refs[8]
        copies = [
            pltpu.make_async_copy(source, target, sems.at[n])
            for n, (source, target) in enumerate(zip(sources, held))
        ]
        for copy in copies:
            copy.start()
        copies[0].wait()
        front_ref, green_ref, field_ref = held
    else:
        front_ref, green_ref, field_ref, own_ref, other_ref = refs
    pairs = front_ref.shape[0] // 2
    re = front_ref[pl.ds(0, pairs, stride=2), :]
    im = front_ref[pl.ds(1, pairs, stride=2), :]
    other_re = swap_orbitals(re, orbits)
    other_im = swap_orbitals(im, orbits)
    square_re = re * re - im * im
    square_im = 2.0 * re * im
    sigma_re = square_re * other_re + square_im * other_im
    sigma_im = square_im * other_re - square_re * other_im
    left_re = split(jnp.concatenate([sigma_re, re], axis=1))
    left_im = split(jnp.concatenate([sigma_im, im], axis=1))
    depth = green_ref.shape[0] // 4
    first = core_ref[0] == 0
    if loads:
        copies[1].wait()
        copies[2].wait()

    def history(half, part):
        pick = pl.ds(2 * half + part, depth, stride=4)
        return jnp.concatenate([green_ref[pick, :], field_ref[pick, :]], axis=0)

    right_re = split(jnp.concatenate([history(0, 0), history(1, 0)], axis=1))
    right_im = split(jnp.concatenate([history(0, 1), history(1, 1)], axis=1))
    image_re = dot3(left_re, right_re) - dot3(left_im, right_im)
    image_im = dot3(left_re, right_im) + dot3(left_im, right_re)
    lanes = own_ref.shape[1]
    for part, image in ((0, image_re), (1, image_im)):
        low, high = image[:, :lanes], image[:, lanes:]
        own = jnp.where(first, low, high)
        other = jnp.where(first, high, low)
        for place, front in enumerate(order):
            here = pl.ds(place * 2 * orbits + part, orbits, stride=2)
            there = slice(front * orbits, (front + 1) * orbits)
            own_ref[here, :] = own[there]
            other_ref[here, :] = other[there]


def collide(core, front, green, field, orbits, order, loads):
    block = jax.ShapeDtypeStruct(front.shape, jnp.float32)
    vmem = pl.BlockSpec(memory_space=pltpu.VMEM)
    taken = pl.BlockSpec(memory_space=pltpu.HBM) if loads else vmem
    operands = (front, green, field)
    return pl.pallas_call(
        functools.partial(collide_kernel, orbits, order, loads),
        out_shape=(block, block),
        in_specs=[pl.BlockSpec(memory_space=pltpu.SMEM)] + [taken] * 3,
        out_specs=(vmem, vmem),
        scratch_shapes=[pltpu.VMEM(x.shape, x.dtype) for x in operands]
        + [pltpu.SemaphoreType.DMA((3,))] if loads else [],
        compiler_params=pltpu.CompilerParams(vmem_limit_bytes=(60 if loads else 12) << 20),
        name="collide",
    )(core, *operands)


def per_device(turn, ys, zs, front_init, green_hist, field_hist):
    fronts, orbits, parts, width = front_init.shape
    rows = fronts * orbits * parts
    init = front_init.reshape(rows, width)

    def tiles(history):
        times, inner, _, lanes = history.shape
        return history.reshape(times, inner, parts, lanes // width, width).transpose(
            0, 1, 3, 2, 4).reshape(-1, width)

    green, field = tiles(green_hist), tiles(field_hist)
    core = lax.axis_index("core").astype(jnp.int32).reshape(1)
    shift = zs // 2
    order = [x * ys + (y + shift) % ys for x in range(fronts // ys) for y in range(ys)]
    mine = lax.axis_index("xh") * zs + lax.axis_index("z")
    start = lax.dynamic_slice_in_dim(init, mine * (rows // fronts), rows // fronts, 0)
    current = init
    for sweep in range(ITERS):
        own, other = collide(core, current, green, field, orbits, order, sweep == 0)
        chip = own + lax.ppermute(other, "core", [(0, 1), (1, 0)])
        spread = lax.all_to_all(chip.reshape(fronts, -1, width), A, 0, 0, tiled=True)
        if sweep == 0:
            start, spread = lax.optimization_barrier((start, spread))
        turned = lax.ppermute(jnp.sum(spread, axis=0), EVERY, turn)
        piece = start + STEP_WEIGHT * turned
        copies = jnp.broadcast_to(piece[None], (fronts,) + piece.shape)
        current = lax.all_to_all(copies, B, 0, 0, tiled=True).reshape(rows, width)
    return current.reshape(front_init.shape)


def solution(mesh):
    xls, ys, cores, xhs, zs = 2, 8, 2, 2, 8
    fine = Mesh(mesh.devices.reshape(xls, ys, cores, xhs, zs), EVERY)

    def place(xl, y, core, xh, z):
        return (((xl * ys + y) * cores + core) * xhs + xh) * zs + z

    turn = [
        (place(xl, y, core, xh, z), place(xh, z, core, xl, (y + zs // 2) % zs))
        for xl in range(xls) for y in range(ys) for core in range(cores)
        for xh in range(xhs) for z in range(zs)
    ]
    return jax.shard_map(
        functools.partial(per_device, turn, ys, zs),
        mesh=fine,
        in_specs=(
            P(None, None, None, ("xl", "y", "core")),
            P(("xl", "y", "core"), None, None, B),
            P(("xl", "y", "core"), None, None, B),
        ),
        out_specs=P(None, None, None, ("xl", "y", "core")),
        check_vma=False,
    )
```

```python
import functools

import jax
import jax.numpy as jnp
from jax import lax
from jax.experimental import pallas as pl
from jax.experimental.pallas import tpu as pltpu
from jax.sharding import Mesh, PartitionSpec as P

ITERS = 2
STEP_WEIGHT = 0.5

A = ("xl", "y")
B = ("xh", "z")
EVERY = ("xl", "y", "core", "xh", "z")


def split(value):
    high = value.astype(jnp.bfloat16)
    low = (value - high.astype(jnp.float32)).astype(jnp.bfloat16)
    return high, low


def dot3(left, right):
    def one(x, y):
        return jnp.dot(x, y, preferred_element_type=jnp.float32)
    return one(left[0], right[0]) + (one(left[0], right[1]) + one(left[1], right[0]))


def swap_orbitals(value, orbits):
    rows, lanes = value.shape
    row = lax.broadcasted_iota(jnp.int32, value.shape, 0)
    lane = lax.broadcasted_iota(jnp.int32, value.shape, 1)
    step = 1
    while step < orbits:
        row_bit = (row // step) % 2
        lane_bit = (lane // step) % 2
        up = pltpu.roll(pltpu.roll(value, step, 1), rows - step, 0)
        down = pltpu.roll(pltpu.roll(value, lanes - step, 1), step, 0)
        value = jnp.where(row_bit == lane_bit, value, jnp.where(row_bit == 0, up, down))
        step *= 2
    return value


def collide_kernel(orbits, order, loads, place_ref, *refs):
    if loads:
        sources, (own_ref, other_ref, piece_ref), held, sems = refs[:3], refs[3:6], refs[6:9], refs[9]
        copies = [
            pltpu.make_async_copy(source, target, sems.at[n])
            for n, (source, target) in enumerate(zip(sources, held))
        ]
        for copy in copies:
            copy.start()
        copies[0].wait()
        front_ref, green_ref, field_ref = held
        piece = piece_ref.shape[0]
        piece_ref[...] = front_ref[pl.ds(pl.multiple_of(place_ref[1] * piece, piece), piece), :]
    else:
        front_ref, green_ref, field_ref, own_ref, other_ref = refs
    pairs = front_ref.shape[0] // 2
    re = front_ref[pl.ds(0, pairs, stride=2), :]
    im = front_ref[pl.ds(1, pairs, stride=2), :]
    other_re = swap_orbitals(re, orbits)
    other_im = swap_orbitals(im, orbits)
    square_re = re * re - im * im
    square_im = 2.0 * re * im
    sigma_re = square_re * other_re + square_im * other_im
    sigma_im = square_im * other_re - square_re * other_im
    left_re = split(jnp.concatenate([sigma_re, re], axis=1))
    left_im = split(jnp.concatenate([sigma_im, im], axis=1))
    depth = green_ref.shape[0] // 4
    first = place_ref[0] == 0
    if loads:
        copies[1].wait()
        copies[2].wait()

    def history(half, part):
        pick = pl.ds(2 * half + part, depth, stride=4)
        return jnp.concatenate([green_ref[pick, :], field_ref[pick, :]], axis=0)

    right_re = split(jnp.concatenate([history(0, 0), history(1, 0)], axis=1))
    right_im = split(jnp.concatenate([history(0, 1), history(1, 1)], axis=1))
    image_re = dot3(left_re, right_re) - dot3(left_im, right_im)
    image_im = dot3(left_re, right_im) + dot3(left_im, right_re)
    lanes = own_ref.shape[1]
    for part, image in ((0, image_re), (1, image_im)):
        low, high = image[:, :lanes], image[:, lanes:]
        own = jnp.where(first, low, high)
        other = jnp.where(first, high, low)
        for place, front in enumerate(order):
            here = pl.ds(place * 2 * orbits + part, orbits, stride=2)
            there = slice(front * orbits, (front + 1) * orbits)
            own_ref[here, :] = own[there]
            other_ref[here, :] = other[there]


def collide(place, front, green, field, orbits, order, loads):
    block = jax.ShapeDtypeStruct(front.shape, jnp.float32)
    piece = ()
    if loads:
        piece = (jax.ShapeDtypeStruct((2 * orbits, front.shape[1]), jnp.float32),)
    vmem = pl.BlockSpec(memory_space=pltpu.VMEM)
    taken = pl.BlockSpec(memory_space=pltpu.HBM) if loads else vmem
    operands = (front, green, field)
    if loads:
        operands = tuple(pltpu.with_memory_space_constraint(x, pltpu.HBM) for x in operands)
    return pl.pallas_call(
        functools.partial(collide_kernel, orbits, order, loads),
        out_shape=(block, block) + piece,
        in_specs=[pl.BlockSpec(memory_space=pltpu.SMEM)] + [taken] * 3,
        out_specs=(vmem,) * (2 + len(piece)),
        scratch_shapes=[pltpu.VMEM(x.shape, x.dtype) for x in operands]
        + [pltpu.SemaphoreType.DMA((3,))] if loads else [],
        compiler_params=pltpu.CompilerParams(vmem_limit_bytes=12 << 20),
        name="collide",
    )(place, *operands)


def per_device(turn, ys, zs, front_init, green_hist, field_hist):
    fronts, orbits, parts, width = front_init.shape
    rows = fronts * orbits * parts
    init = front_init.reshape(rows, width)

    def tiles(history):
        times, inner, _, lanes = history.shape
        return history.reshape(times, inner, parts, lanes // width, width).transpose(
            0, 1, 3, 2, 4).reshape(-1, width)

    green, field = tiles(green_hist), tiles(field_hist)
    shift = zs // 2
    order = [x * ys + (y + shift) % ys for x in range(fronts // ys) for y in range(ys)]
    mine = lax.axis_index("xh") * zs + lax.axis_index("z")
    place = jnp.stack([lax.axis_index("core"), mine]).astype(jnp.int32)
    current = init
    for sweep in range(ITERS):
        own, other, *first = collide(place, current, green, field, orbits, order, sweep == 0)
        start = first[0] if first else start
        chip = own + lax.ppermute(other, "core", [(0, 1), (1, 0)])
        spread = lax.all_to_all(chip.reshape(fronts, -1, width), A, 0, 0, tiled=True)
        turned = lax.ppermute(jnp.sum(spread, axis=0), EVERY, turn)
        piece = start + STEP_WEIGHT * turned
        copies = jnp.broadcast_to(piece[None], (fronts,) + piece.shape)
        current = lax.all_to_all(copies, B, 0, 0, tiled=True).reshape(rows, width)
    return current.reshape(front_init.shape)


def solution(mesh):
    xls, ys, cores, xhs, zs = 2, 8, 2, 2, 8
    fine = Mesh(mesh.devices.reshape(xls, ys, cores, xhs, zs), EVERY)

    def place(xl, y, core, xh, z):
        return (((xl * ys + y) * cores + core) * xhs + xh) * zs + z

    turn = [
        (place(xl, y, core, xh, z), place(xh, z, core, xl, (y + zs // 2) % zs))
        for xl in range(xls) for y in range(ys) for core in range(cores)
        for xh in range(xhs) for z in range(zs)
    ]
    return jax.shard_map(
        functools.partial(per_device, turn, ys, zs),
        mesh=fine,
        in_specs=(
            P(None, None, None, ("xl", "y", "core")),
            P(("xl", "y", "core"), None, None, B),
            P(("xl", "y", "core"), None, None, B),
        ),
        out_specs=P(None, None, None, ("xl", "y", "core")),
        check_vma=False,
    )
```

```python
import functools

import jax
import jax.numpy as jnp
from jax import lax
from jax.experimental import pallas as pl
from jax.experimental.pallas import tpu as pltpu
from jax.sharding import Mesh, PartitionSpec as P


STEP_WEIGHT = 0.5

A = ("xl", "y")
B = ("xh", "z")
EVERY = ("xl", "y", "core", "xh", "z")


def split(value):
    high = value.astype(jnp.bfloat16)
    low = (value - high.astype(jnp.float32)).astype(jnp.bfloat16)
    return high, low


def dot3(left, right):
    def one(x, y):
        return jnp.dot(x, y, preferred_element_type=jnp.float32)

    return one(left[0], right[0]) + (one(left[0], right[1]) + one(left[1], right[0]))


def swap_orbitals(value, orbits):
    rows, lanes = value.shape
    row = lax.broadcasted_iota(jnp.int32, value.shape, 0)
    lane = lax.broadcasted_iota(jnp.int32, value.shape, 1)
    step = 1
    while step < orbits:
        row_bit = (row // step) % 2
        lane_bit = (lane // step) % 2
        up = pltpu.roll(pltpu.roll(value, step, 1), rows - step, 0)
        down = pltpu.roll(pltpu.roll(value, lanes - step, 1), step, 0)
        value = jnp.where(row_bit == lane_bit, value, jnp.where(row_bit == 0, up, down))
        step *= 2
    return value


def sigma_pair(re, im, orbits):
    other_re = swap_orbitals(re, orbits)
    other_im = swap_orbitals(im, orbits)
    square_re = re * re - im * im
    square_im = 2.0 * re * im
    return (
        square_re * other_re + square_im * other_im,
        square_im * other_re - square_re * other_im,
    )


def history(refs, part):
    depth = refs[0].shape[0] // 4
    halves = [
        jnp.concatenate([ref[pl.ds(2 * half + part, depth, stride=4), :] for ref in refs], axis=0)
        for half in range(2)
    ]
    return jnp.concatenate(halves, axis=1)


def image_of(left_re, left_im, refs):
    left_re, left_im = split(left_re), split(left_im)
    right_re, right_im = split(history(refs, 0)), split(history(refs, 1))
    return (
        dot3(left_re, right_re) - dot3(left_im, right_im),
        dot3(left_re, right_im) + dot3(left_im, right_re),
    )


def put(target_ref, part, image, orbits, order):
    lanes = target_ref.shape[1]
    for half in range(2):
        for place, front in enumerate(order):
            first = (half * len(order) + place) * 2 * orbits + part
            target_ref[pl.ds(first, orbits, stride=2), :] = image[
                front * orbits:(front + 1) * orbits, half * lanes:(half + 1) * lanes]


def first_kernel(orbits, order, init_ref, green_ref, field_ref,
                 own_ref, other_ref, near_ref, last_ref, init, green, field, sems):
    copies = [
        pltpu.make_async_copy(source, target, sems.at[n])
        for n, (source, target) in enumerate(
            ((init_ref, init), (green_ref, green), (field_ref, field)))
    ]
    for copy in copies:
        copy.start()
    core, xh, z = (lax.axis_index(axis) for axis in ("core", "xh", "z"))
    fronts = len(order)
    piece = 2 * orbits
    rows = init.shape[0]

    def front(index):
        return init[pl.ds(pl.multiple_of(index * piece, piece), piece), :]

    copies[0].wait()
    near_ref[...] = front(core * fronts + z)
    last_ref[...] = front(xh * fronts + z)
    other_ref[rows:, :] = front((1 - core) * fronts + z)
    re = init[pl.ds(0, rows // 2, stride=2), :]
    im = init[pl.ds(1, rows // 2, stride=2), :]
    sigma_re, sigma_im = sigma_pair(re, im, orbits)
    left_re = jnp.concatenate([sigma_re, re], axis=1)
    left_im = jnp.concatenate([sigma_im, im], axis=1)
    copies[1].wait()
    copies[2].wait()
    images = image_of(left_re, left_im, (green, field))
    cut = rows // 4
    for part, image in enumerate(images):
        low, high = image[:cut], image[cut:]
        put(own_ref, part, jnp.where(core == 0, low, high), orbits, order)
        put(other_ref, part, jnp.where(core == 0, high, low), orbits, order)


def second_kernel(orbits, order, front_ref, green_ref, field_ref, green_far, field_far, out_ref):
    core = lax.axis_index("core")
    half_rows = front_ref.shape[0] // 2

    def part_of(part):
        halves = [
            front_ref[pl.ds(half * half_rows + part, half_rows // 2, stride=2), :]
            for half in range(2)
        ]
        return jnp.where(core == 0, halves[0], halves[1]), jnp.where(core == 0, halves[1], halves[0])

    left_re, left_im = [], []
    for re, im in zip(part_of(0), part_of(1)):
        sigma_re, sigma_im = sigma_pair(re, im, orbits)
        left_re += [sigma_re, re]
        left_im += [sigma_im, im]
    images = image_of(
        jnp.concatenate(left_re, axis=1), jnp.concatenate(left_im, axis=1),
        (green_ref, field_ref, green_far, field_far))
    for part, image in enumerate(images):
        put(out_ref, part, image, orbits, order)


VMEM = pl.BlockSpec(memory_space=pltpu.VMEM)
LIMIT = pltpu.CompilerParams(vmem_limit_bytes=12 << 20)


def first_collide(init, green, field, orbits, order):
    rows, width = init.shape
    operands = [pltpu.with_memory_space_constraint(x, pltpu.HBM) for x in (init, green, field)]
    return pl.pallas_call(
        functools.partial(first_kernel, orbits, order),
        out_shape=[
            jax.ShapeDtypeStruct((n, width), jnp.float32)
            for n in (rows, rows + 2 * orbits, 2 * orbits, 2 * orbits)
        ],
        in_specs=[pl.BlockSpec(memory_space=pltpu.HBM)] * 3,
        out_specs=[VMEM] * 4,
        scratch_shapes=[pltpu.VMEM(x.shape, x.dtype) for x in (init, green, field)]
        + [pltpu.SemaphoreType.DMA((3,))],
        compiler_params=LIMIT,
        name="first_collide",
    )(*operands)


def second_collide(front, histories, orbits, order):
    return pl.pallas_call(
        functools.partial(second_kernel, orbits, order),
        out_shape=jax.ShapeDtypeStruct(front.shape, jnp.float32),
        in_specs=[VMEM] * 5,
        out_specs=VMEM,
        compiler_params=LIMIT,
        name="second_collide",
    )(front, *histories)


def per_device(turns, ys, zs, front_init, green_hist, field_hist):
    return corrector(turns, ys, zs, front_init, green_hist, field_hist)


def corrector(turns, ys, zs, front_init, green_hist, field_hist):
    fronts, orbits, parts, width = front_init.shape
    rows = fronts * orbits * parts
    init = front_init.reshape(rows, width)

    def tiles(history):
        times, inner, _, lanes = history.shape
        return history.reshape(times, inner, parts, lanes // width, width).transpose(
            0, 1, 3, 2, 4).reshape(-1, width)

    def swap(value):
        return lax.ppermute(value, "core", [(0, 1), (1, 0)])

    def reduced(partial_sum):
        spread = lax.all_to_all(partial_sum.reshape(fronts, -1, width), A, 0, 0, tiled=True)
        return jnp.sum(spread, axis=0)

    def gathered(copies):
        return lax.all_to_all(copies, B, 0, 0, tiled=True).reshape(rows, width)

    def copies_of(start, turned):
        piece = start + STEP_WEIGHT * turned
        return jnp.broadcast_to(piece[None], (fronts,) + piece.shape)

    green, field = tiles(green_hist), tiles(field_hist)
    order = [(y + zs // 2) % zs for y in range(ys)]
    own, other, near, last = first_collide(init, green, field, orbits, order)
    arrived = swap(other)
    piece = reduced(own + arrived[:rows])
    near = jnp.where(lax.axis_index("xh") == lax.axis_index("core"), near, arrived[rows:])
    green_late, field_late, piece = lax.optimization_barrier((green, field, piece))
    turned = lax.ppermute(piece, EVERY, turns[0])
    green_far = swap(green_late)
    field_far = swap(field_late)
    copies = copies_of(near, turned)
    green_far, field_far, copies = lax.optimization_barrier((green_far, field_far, copies))
    current = gathered(copies)
    image = second_collide(current, (green, field, green_far, field_far), orbits, order)
    turned = lax.ppermute(reduced(image), EVERY, turns[1])
    return gathered(copies_of(last, turned)).reshape(front_init.shape)


def solution(mesh):
    xls, ys, cores, xhs, zs = 2, 8, 2, 2, 8
    fine = Mesh(mesh.devices.reshape(xls, ys, cores, xhs, zs), EVERY)

    def place(xl, y, core, xh, z):
        return (((xl * ys + y) * cores + core) * xhs + xh) * zs + z

    everyone = [
        (xl, y, core, xh, z)
        for xl in range(xls) for y in range(ys) for core in range(cores)
        for xh in range(xhs) for z in range(zs)
    ]
    turns = [
        [(place(xl, y, core, xh, z), place(xh, z, core, xl, (y + zs // 2) % zs))
         for xl, y, core, xh, z in everyone],
        [(place(xl, y, core, xh, z), place(xh, z, xl, core, (y + zs // 2) % zs))
         for xl, y, core, xh, z in everyone],
    ]
    return jax.shard_map(
        functools.partial(per_device, turns, ys, zs),
        mesh=fine,
        in_specs=(
            P(None, None, None, ("xl", "y", "core")),
            P(("xl", "y", "core"), None, None, B),
            P(("xl", "y", "core"), None, None, B),
        ),
        out_specs=P(None, None, None, ("xl", "y", "core")),
        check_vma=False,
    )
```

```python
import functools

import jax
import jax.numpy as jnp
from jax import lax
from jax.experimental import pallas as pl
from jax.experimental.pallas import tpu as pltpu
from jax.sharding import Mesh, PartitionSpec as P


STEP_WEIGHT = 0.5

A = ("xl", "y")
B = ("xh", "z")
EVERY = ("xl", "y", "core", "xh", "z")


def split(value):
    high = value.astype(jnp.bfloat16)
    low = (value - high.astype(jnp.float32)).astype(jnp.bfloat16)
    return high, low


def swap_orbitals(value, orbits):
    rows, lanes = value.shape
    row = lax.broadcasted_iota(jnp.int32, value.shape, 0)
    lane = lax.broadcasted_iota(jnp.int32, value.shape, 1)
    step = 1
    while step < orbits:
        row_bit = (row // step) % 2
        lane_bit = (lane // step) % 2
        up = pltpu.roll(pltpu.roll(value, step, 1), rows - step, 0)
        down = pltpu.roll(pltpu.roll(value, lanes - step, 1), step, 0)
        value = jnp.where(row_bit == lane_bit, value, jnp.where(row_bit == 0, up, down))
        step *= 2
    return value


def sigma_pair(re, im, orbits):
    other_re = swap_orbitals(re, orbits)
    other_im = swap_orbitals(im, orbits)
    square_re = re * re - im * im
    square_im = 2.0 * re * im
    return (
        square_re * other_re + square_im * other_im,
        square_im * other_re - square_re * other_im,
    )


def history(refs, part):
    depth = refs[0].shape[0] // 4
    halves = [
        jnp.concatenate([ref[pl.ds(2 * half + part, depth, stride=4), :] for ref in refs], axis=0)
        for half in range(2)
    ]
    return jnp.concatenate(halves, axis=1)


def image_of(left_re, left_im, refs):
    (re_high, re_low), (im_high, im_low) = split(left_re), split(left_im)
    right_re, right_im = split(history(refs, 0)), split(history(refs, 1))

    def one(re_first, im_first, first, second):
        left = jnp.concatenate(
            [re_first[0], im_first[0], re_first[0], im_first[0], re_first[1], im_first[1]], axis=1)
        right = jnp.concatenate(
            [first[0], second[0], first[1], second[1], first[0], second[0]], axis=0)
        return jnp.dot(left, right, preferred_element_type=jnp.float32)

    re, im = (re_high, re_low), (im_high, im_low)
    return one(re, (-im_high, -im_low), right_re, right_im), one(re, im, right_im, right_re)


def put(target_ref, part, image, orbits, order):
    lanes = target_ref.shape[1]
    for half in range(2):
        for place, front in enumerate(order):
            first = (half * len(order) + place) * 2 * orbits + part
            target_ref[pl.ds(first, orbits, stride=2), :] = image[
                front * orbits:(front + 1) * orbits, half * lanes:(half + 1) * lanes]


def first_kernel(orbits, order, init_ref, green_ref, field_ref,
                 own_ref, other_ref, near_ref, last_ref, init, green, field, sems):
    copies = [
        pltpu.make_async_copy(source, target, sems.at[n])
        for n, (source, target) in enumerate(
            ((init_ref, init), (green_ref, green), (field_ref, field)))
    ]
    for copy in copies:
        copy.start()
    core, xl, xh, z = (lax.axis_index(axis) for axis in ("core", "xl", "xh", "z"))
    fronts = len(order)
    piece = 2 * orbits
    rows = init.shape[0]

    def front(index):
        return init[pl.ds(pl.multiple_of(index * piece, piece), piece), :]

    copies[0].wait()
    near_ref[...] = front(core * fronts + z)
    last_ref[...] = front((core + 1 + xh + xl) % 2 * fronts + z)
    other_ref[rows:, :] = front((1 - core) * fronts + z)
    re = init[pl.ds(0, rows // 2, stride=2), :]
    im = init[pl.ds(1, rows // 2, stride=2), :]
    sigma_re, sigma_im = sigma_pair(re, im, orbits)
    left_re = jnp.concatenate([sigma_re, re], axis=1)
    left_im = jnp.concatenate([sigma_im, im], axis=1)
    copies[1].wait()
    copies[2].wait()
    images = image_of(left_re, left_im, (green, field))
    cut = rows // 4
    for part, image in enumerate(images):
        low, high = image[:cut], image[cut:]
        put(own_ref, part, jnp.where(core == 0, low, high), orbits, order)
        put(other_ref, part, jnp.where(core == 0, high, low), orbits, order)


def second_kernel(orbits, order, front_ref, green_ref, field_ref, green_far, field_far, out_ref):
    core = lax.axis_index("core")
    half_rows = front_ref.shape[0] // 2

    def part_of(part):
        halves = [
            front_ref[pl.ds(half * half_rows + part, half_rows // 2, stride=2), :]
            for half in range(2)
        ]
        return jnp.where(core == 0, halves[0], halves[1]), jnp.where(core == 0, halves[1], halves[0])

    left_re, left_im = [], []
    for re, im in zip(part_of(0), part_of(1)):
        sigma_re, sigma_im = sigma_pair(re, im, orbits)
        left_re += [sigma_re, re]
        left_im += [sigma_im, im]
    images = image_of(
        jnp.concatenate(left_re, axis=1), jnp.concatenate(left_im, axis=1),
        (green_ref, field_ref, green_far, field_far))
    lanes = out_ref.shape[1]
    straight = (core + 1 + lax.axis_index("xh")) % 2 == 0
    for part, image in enumerate(images):
        low, high = image[:, :lanes], image[:, lanes:]
        first, second = jnp.where(straight, low, high), jnp.where(straight, high, low)
        put(out_ref, part, jnp.concatenate([first, second], axis=1), orbits, order)


VMEM = pl.BlockSpec(memory_space=pltpu.VMEM)
LIMIT = pltpu.CompilerParams(vmem_limit_bytes=12 << 20)


def first_collide(init, green, field, orbits, order):
    rows, width = init.shape
    operands = [pltpu.with_memory_space_constraint(x, pltpu.HBM) for x in (init, green, field)]
    return pl.pallas_call(
        functools.partial(first_kernel, orbits, order),
        out_shape=[
            jax.ShapeDtypeStruct((n, width), jnp.float32)
            for n in (rows, rows + 2 * orbits, 2 * orbits, 2 * orbits)
        ],
        in_specs=[pl.BlockSpec(memory_space=pltpu.HBM)] * 3,
        out_specs=[VMEM] * 4,
        scratch_shapes=[pltpu.VMEM(x.shape, x.dtype) for x in (init, green, field)]
        + [pltpu.SemaphoreType.DMA((3,))],
        compiler_params=LIMIT,
        name="first_collide",
    )(*operands)


def second_collide(front, histories, orbits, order):
    return pl.pallas_call(
        functools.partial(second_kernel, orbits, order),
        out_shape=jax.ShapeDtypeStruct(front.shape, jnp.float32),
        in_specs=[VMEM] * 5,
        out_specs=VMEM,
        compiler_params=LIMIT,
        name="second_collide",
    )(front, *histories)


def per_device(turns, ys, zs, front_init, green_hist, field_hist):
    return corrector(turns, ys, zs, front_init, green_hist, field_hist)


def corrector(turns, ys, zs, front_init, green_hist, field_hist):
    fronts, orbits, parts, width = front_init.shape
    rows = fronts * orbits * parts
    init = front_init.reshape(rows, width)

    def tiles(history):
        times, inner, _, lanes = history.shape
        return history.reshape(times, inner, parts, lanes // width, width).transpose(
            0, 1, 3, 2, 4).reshape(-1, width)

    def swap(value):
        return lax.ppermute(value, "core", [(0, 1), (1, 0)])

    def reduced(partial_sum):
        spread = lax.all_to_all(partial_sum.reshape(fronts, -1, width), A, 0, 0, tiled=True)
        return jnp.sum(spread, axis=0)

    def gathered(copies):
        return lax.all_to_all(copies, B, 0, 0, tiled=True).reshape(rows, width)

    def copies_of(start, turned):
        piece = start + STEP_WEIGHT * turned
        return jnp.broadcast_to(piece[None], (fronts,) + piece.shape)

    green, field = tiles(green_hist), tiles(field_hist)
    order = [(y + zs // 2) % zs for y in range(ys)]
    own, other, near, last = first_collide(init, green, field, orbits, order)
    arrived = swap(other)
    piece = reduced(own + arrived[:rows])
    near = jnp.where(lax.axis_index("xh") == lax.axis_index("core"), near, arrived[rows:])
    green_late, field_late, piece = lax.optimization_barrier((green, field, piece))
    turned = lax.ppermute(piece, EVERY, turns[0])
    green_far = swap(green_late)
    field_far = swap(field_late)
    copies = copies_of(near, turned)
    green_far, field_far, copies = lax.optimization_barrier((green_far, field_far, copies))
    current = gathered(copies)
    image = second_collide(current, (green, field, green_far, field_far), orbits, order)
    turned = lax.ppermute(reduced(image), EVERY, turns[1])
    final = gathered(copies_of(last, turned)).reshape(2, rows // 2, width)
    straight = (lax.axis_index("core") + 1 + lax.axis_index("xl")) % 2 == 0
    return jnp.where(straight, final, final[::-1]).reshape(front_init.shape)


def solution(mesh):
    xls, ys, cores, xhs, zs = 2, 8, 2, 2, 8
    fine = Mesh(mesh.devices.reshape(xls, ys, cores, xhs, zs), EVERY)

    def place(xl, y, core, xh, z):
        return (((xl * ys + y) * cores + core) * xhs + xh) * zs + z

    everyone = [
        (xl, y, core, xh, z)
        for xl in range(xls) for y in range(ys) for core in range(cores)
        for xh in range(xhs) for z in range(zs)
    ]
    turns = [
        [(place(xl, y, core, xh, z), place(xh, z, core, xl, (y + zs // 2) % zs))
         for xl, y, core, xh, z in everyone],
        [(place(xl, y, core, xh, z), place(xh, z, core if xl != xh else 1 - core, xl, (y + zs // 2) % zs))
         for xl, y, core, xh, z in everyone],
    ]
    return jax.shard_map(
        functools.partial(per_device, turns, ys, zs),
        mesh=fine,
        in_specs=(
            P(None, None, None, ("xl", "y", "core")),
            P(("xl", "y", "core"), None, None, B),
            P(("xl", "y", "core"), None, None, B),
        ),
        out_specs=P(None, None, None, ("xl", "y", "core")),
        check_vma=False,
    )
```

```python
import functools

import jax
import jax.numpy as jnp
from jax import lax
from jax.experimental import pallas as pl
from jax.experimental.pallas import tpu as pltpu
from jax.sharding import Mesh, PartitionSpec as P


STEP_WEIGHT = 0.5

A = ("xl", "y")
B = ("xh", "z")
EVERY = ("xl", "y", "core", "xh", "z")


def split(value):
    high = value.astype(jnp.bfloat16)
    low = (value - high.astype(jnp.float32)).astype(jnp.bfloat16)
    return high, low


def swap_orbitals(value, orbits):
    rows, lanes = value.shape
    row = lax.broadcasted_iota(jnp.int32, value.shape, 0)
    lane = lax.broadcasted_iota(jnp.int32, value.shape, 1)
    step = 1
    while step < orbits:
        row_bit = (row // step) % 2
        lane_bit = (lane // step) % 2
        up = pltpu.roll(pltpu.roll(value, step, 1), rows - step, 0)
        down = pltpu.roll(pltpu.roll(value, lanes - step, 1), step, 0)
        value = jnp.where(row_bit == lane_bit, value, jnp.where(row_bit == 0, up, down))
        step *= 2
    return value


def sigma_pair(re, im, orbits):
    other_re = swap_orbitals(re, orbits)
    other_im = swap_orbitals(im, orbits)
    square_re = re * re - im * im
    square_im = 2.0 * re * im
    return (
        square_re * other_re + square_im * other_im,
        square_im * other_re - square_re * other_im,
    )


def history(refs, part):
    depth = refs[0].shape[0] // 4
    halves = [
        jnp.concatenate([ref[pl.ds(2 * half + part, depth, stride=4), :] for ref in refs], axis=0)
        for half in range(2)
    ]
    return jnp.concatenate(halves, axis=1)


def image_of(left_re, left_im, refs):
    (re_high, re_low), (im_high, im_low) = split(left_re), split(left_im)
    right_re, right_im = split(history(refs, 0)), split(history(refs, 1))

    def one(re_first, im_first, first, second):
        left = jnp.concatenate(
            [re_first[0], im_first[0], re_first[0], im_first[0], re_first[1], im_first[1]], axis=1)
        right = jnp.concatenate(
            [first[0], second[0], first[1], second[1], first[0], second[0]], axis=0)
        return jnp.dot(left, right, preferred_element_type=jnp.float32)

    re, im = (re_high, re_low), (im_high, im_low)
    return one(re, (-im_high, -im_low), right_re, right_im), one(re, im, right_im, right_re)


def put(target_ref, part, image, orbits, order):
    lanes = target_ref.shape[1]
    for half in range(2):
        for place, front in enumerate(order):
            first = (half * len(order) + place) * 2 * orbits + part
            target_ref[pl.ds(first, orbits, stride=2), :] = image[
                front * orbits:(front + 1) * orbits, half * lanes:(half + 1) * lanes]


def half_image(init_ref, green_ref, field_ref, orbits, lower):
    pairs = init_ref.shape[0] // 4
    re, im = (
        jnp.where(lower, init_ref[pl.ds(part, pairs, stride=2), :],
                  init_ref[pl.ds(2 * pairs + part, pairs, stride=2), :])
        for part in range(2)
    )
    sigma_re, sigma_im = sigma_pair(re, im, orbits)
    return image_of(
        jnp.concatenate([sigma_re, re], axis=1), jnp.concatenate([sigma_im, im], axis=1),
        (green_ref, field_ref))


def first_kernel(orbits, order, init_ref, green_ref, field_ref,
                 other_ref, near_ref, last_ref, flag_ref, init, green, field, sems):
    copies = [
        pltpu.make_async_copy(source, target, sems.at[n])
        for n, (source, target) in enumerate(
            ((init_ref, init), (green_ref, green), (field_ref, field)))
    ]
    for copy in copies:
        copy.start()
    core, xl, xh, z = (lax.axis_index(axis) for axis in ("core", "xl", "xh", "z"))
    fronts = len(order)
    piece = 2 * orbits
    rows = init.shape[0]
    flag_ref[...] = jnp.full(flag_ref.shape, (core + 1 + xl) % 2, jnp.int32)

    def front(index):
        return init[pl.ds(pl.multiple_of(index * piece, piece), piece), :]

    for copy in copies:
        copy.wait()
    near_ref[...] = front(core * fronts + z)
    last_ref[...] = front((core + 1 + xh + xl) % 2 * fronts + z)
    other_ref[rows:, :] = front((1 - core) * fronts + z)
    for part, image in enumerate(half_image(init, green, field, orbits, core == 1)):
        put(other_ref, part, image, orbits, order)


def kept_kernel(orbits, order, init_ref, green_ref, field_ref, own_ref):
    core = lax.axis_index("core")
    for part, image in enumerate(half_image(init_ref, green_ref, field_ref, orbits, core == 0)):
        put(own_ref, part, image, orbits, order)


def second_kernel(orbits, order, front_ref, green_ref, field_ref, green_far, field_far, out_ref):
    core = lax.axis_index("core")
    half_rows = front_ref.shape[0] // 2

    def part_of(part):
        halves = [
            front_ref[pl.ds(half * half_rows + part, half_rows // 2, stride=2), :]
            for half in range(2)
        ]
        return jnp.where(core == 0, halves[0], halves[1]), jnp.where(core == 0, halves[1], halves[0])

    left_re, left_im = [], []
    for re, im in zip(part_of(0), part_of(1)):
        sigma_re, sigma_im = sigma_pair(re, im, orbits)
        left_re += [sigma_re, re]
        left_im += [sigma_im, im]
    images = image_of(
        jnp.concatenate(left_re, axis=1), jnp.concatenate(left_im, axis=1),
        (green_ref, field_ref, green_far, field_far))
    lanes = out_ref.shape[1]
    straight = (core + 1 + lax.axis_index("xh")) % 2 == 0
    for part, image in enumerate(images):
        low, high = image[:, :lanes], image[:, lanes:]
        first, second = jnp.where(straight, low, high), jnp.where(straight, high, low)
        put(out_ref, part, jnp.concatenate([first, second], axis=1), orbits, order)


VMEM = pl.BlockSpec(memory_space=pltpu.VMEM)
LIMIT = pltpu.CompilerParams(vmem_limit_bytes=12 << 20)


def first_collide(init, green, field, orbits, order):
    rows, width = init.shape
    operands = [pltpu.with_memory_space_constraint(x, pltpu.HBM) for x in (init, green, field)]
    return pl.pallas_call(
        functools.partial(first_kernel, orbits, order),
        out_shape=[
            jax.ShapeDtypeStruct((n, width), kind) for n, kind in (
                (rows + 2 * orbits, jnp.float32), (2 * orbits, jnp.float32),
                (2 * orbits, jnp.float32), (8, jnp.int32), (rows, jnp.float32),
                (rows, jnp.float32), (rows, jnp.float32))
        ],
        in_specs=[pl.BlockSpec(memory_space=pltpu.HBM)] * 3,
        out_specs=[VMEM] * 7,
        scratch_shapes=[pltpu.SemaphoreType.DMA((3,))],
        compiler_params=LIMIT,
        name="first_collide",
    )(*operands)


def kept_collide(init, green, field, orbits, order):
    return pl.pallas_call(
        functools.partial(kept_kernel, orbits, order),
        out_shape=jax.ShapeDtypeStruct(init.shape, jnp.float32),
        in_specs=[VMEM] * 3,
        out_specs=VMEM,
        compiler_params=LIMIT,
        cost_estimate=pl.CostEstimate(flops=10**8, bytes_accessed=10**6, transcendentals=0),
        name="kept_collide",
    )(init, green, field)


def second_collide(front, histories, orbits, order):
    return pl.pallas_call(
        functools.partial(second_kernel, orbits, order),
        out_shape=jax.ShapeDtypeStruct(front.shape, jnp.float32),
        in_specs=[VMEM] * 5,
        out_specs=VMEM,
        compiler_params=LIMIT,
        name="second_collide",
    )(front, *histories)


def per_device(turns, ys, zs, front_init, green_hist, field_hist):
    return corrector(turns, ys, zs, front_init, green_hist, field_hist)


def corrector(turns, ys, zs, front_init, green_hist, field_hist):
    fronts, orbits, parts, width = front_init.shape
    rows = fronts * orbits * parts
    init = front_init.reshape(rows, width)

    def tiles(history):
        times, inner, _, lanes = history.shape
        return history.reshape(times, inner, parts, lanes // width, width).transpose(
            0, 1, 3, 2, 4).reshape(-1, width)

    def swap(value):
        return lax.ppermute(value, "core", [(0, 1), (1, 0)])

    def reduced(partial_sum):
        spread = lax.all_to_all(partial_sum.reshape(fronts, -1, width), A, 0, 0, tiled=True)
        return jnp.sum(spread, axis=0)

    def gathered(copies):
        return lax.all_to_all(copies, B, 0, 0, tiled=True).reshape(rows, width)

    def copies_of(start, turned):
        piece = start + STEP_WEIGHT * turned
        return jnp.broadcast_to(piece[None], (fronts,) + piece.shape)

    green, field = tiles(green_hist), tiles(field_hist)
    order = [(y + zs // 2) % zs for y in range(ys)]
    other, near, last, flag, init, green, field = first_collide(
        init, green, field, orbits, order)
    arrived = swap(other)
    own = kept_collide(init, green, field, orbits, order)
    flag = jnp.broadcast_to(flag == 0, (2, rows // 16, 8, width))
    own, flag = lax.optimization_barrier((own, flag))
    piece = reduced(own + arrived[:rows])
    near = jnp.where(lax.axis_index("xh") == lax.axis_index("core"), near, arrived[rows:])
    green_late, field_late, piece = lax.optimization_barrier((green, field, piece))
    turned = lax.ppermute(piece, EVERY, turns[0])
    green_far = swap(green_late)
    field_far = swap(field_late)
    copies = copies_of(near, turned)
    green_far, field_far, copies = lax.optimization_barrier((green_far, field_far, copies))
    current = gathered(copies)
    image = second_collide(current, (green, field, green_far, field_far), orbits, order)
    turned = lax.ppermute(reduced(image), EVERY, turns[1])
    final = gathered(copies_of(last, turned)).reshape(2, -1, 8, width)
    return jnp.where(flag, final, final[::-1]).reshape(front_init.shape)


def solution(mesh):
    xls, ys, cores, xhs, zs = 2, 8, 2, 2, 8
    fine = Mesh(mesh.devices.reshape(xls, ys, cores, xhs, zs), EVERY)

    def place(xl, y, core, xh, z):
        return (((xl * ys + y) * cores + core) * xhs + xh) * zs + z

    everyone = [
        (xl, y, core, xh, z)
        for xl in range(xls) for y in range(ys) for core in range(cores)
        for xh in range(xhs) for z in range(zs)
    ]
    turns = [
        [(place(xl, y, core, xh, z), place(xh, z, core, xl, (y + zs // 2) % zs))
         for xl, y, core, xh, z in everyone],
        [(place(xl, y, core, xh, z), place(xh, z, core if xl != xh else 1 - core, xl, (y + zs // 2) % zs))
         for xl, y, core, xh, z in everyone],
    ]
    return jax.shard_map(
        functools.partial(per_device, turns, ys, zs),
        mesh=fine,
        in_specs=(
            P(None, None, None, ("xl", "y", "core")),
            P(("xl", "y", "core"), None, None, B),
            P(("xl", "y", "core"), None, None, B),
        ),
        out_specs=P(None, None, None, ("xl", "y", "core")),
        check_vma=False,
    )
```

```python
import functools

import jax
import jax.numpy as jnp
from jax import lax
from jax.experimental import pallas as pl
from jax.experimental.pallas import tpu as pltpu
from jax.sharding import Mesh, PartitionSpec as P


STEP_WEIGHT = 0.5

A = ("xl", "y")
B = ("xh", "z")
EVERY = ("xl", "y", "core", "xh", "z")


def split(value):
    high = value.astype(jnp.bfloat16)
    low = (value - high.astype(jnp.float32)).astype(jnp.bfloat16)
    return high, low


def swap_orbitals(value, orbits):
    rows, lanes = value.shape
    row = lax.broadcasted_iota(jnp.int32, value.shape, 0)
    lane = lax.broadcasted_iota(jnp.int32, value.shape, 1)
    step = 1
    while step < orbits:
        row_bit = (row // step) % 2
        lane_bit = (lane // step) % 2
        up = pltpu.roll(pltpu.roll(value, step, 1), rows - step, 0)
        down = pltpu.roll(pltpu.roll(value, lanes - step, 1), step, 0)
        value = jnp.where(row_bit == lane_bit, value, jnp.where(row_bit == 0, up, down))
        step *= 2
    return value


def sigma_pair(re, im, orbits):
    other_re = swap_orbitals(re, orbits)
    other_im = swap_orbitals(im, orbits)
    square_re = re * re - im * im
    square_im = 2.0 * re * im
    return (
        square_re * other_re + square_im * other_im,
        square_im * other_re - square_re * other_im,
    )


def history(refs, part, block):
    depth = block // 4
    halves = [
        jnp.concatenate([
            ref[pl.ds(ref.shape[0] - last * block + 2 * half + part, depth, stride=4), :]
            for ref in refs for last in (2, 1)
        ], axis=0)
        for half in range(2)
    ]
    return jnp.concatenate(halves, axis=1)


def image_of(left_re, left_im, refs, block):
    (re_high, re_low), (im_high, im_low) = split(left_re), split(left_im)
    right_re, right_im = split(history(refs, 0, block)), split(history(refs, 1, block))

    def one(re_first, im_first, first, second):
        left = jnp.concatenate(
            [re_first[0], im_first[0], re_first[0], im_first[0], re_first[1], im_first[1]], axis=1)
        right = jnp.concatenate(
            [first[0], second[0], first[1], second[1], first[0], second[0]], axis=0)
        return jnp.dot(left, right, preferred_element_type=jnp.float32)

    re, im = (re_high, re_low), (im_high, im_low)
    return one(re, (-im_high, -im_low), right_re, right_im), one(re, im, right_im, right_re)


def put(target_ref, part, image, orbits, order):
    lanes = target_ref.shape[1]
    for half in range(2):
        for place, front in enumerate(order):
            first = (half * len(order) + place) * 2 * orbits + part
            target_ref[pl.ds(first, orbits, stride=2), :] = image[
                front * orbits:(front + 1) * orbits, half * lanes:(half + 1) * lanes]


def half_image(init_ref, sent_ref, orbits, lower, block):
    pairs = init_ref.shape[0] // 4
    re, im = (
        jnp.where(lower, init_ref[pl.ds(part, pairs, stride=2), :],
                  init_ref[pl.ds(2 * pairs + part, pairs, stride=2), :])
        for part in range(2)
    )
    sigma_re, sigma_im = sigma_pair(re, im, orbits)
    return image_of(
        jnp.concatenate([sigma_re, re], axis=1), jnp.concatenate([sigma_im, im], axis=1),
        (sent_ref,), block)


def first_kernel(orbits, order, init_ref, green_ref, field_ref,
                 sent_ref, near_ref, last_ref, flag_ref, init, sems):
    block = green_ref.shape[0]
    end = sent_ref.shape[0]
    copies = [
        pltpu.make_async_copy(source, target, sems.at[n])
        for n, (source, target) in enumerate((
            (init_ref, init),
            (green_ref, sent_ref.at[pl.ds(end - 2 * block, block)]),
            (field_ref, sent_ref.at[pl.ds(end - block, block)]),
        ))
    ]
    for copy in copies:
        copy.start()
    core, xl, xh, z = (lax.axis_index(axis) for axis in ("core", "xl", "xh", "z"))
    fronts = len(order)
    piece = 2 * orbits
    rows = init.shape[0]
    flag_ref[...] = jnp.full(flag_ref.shape, (core + 1 + xl) % 2, jnp.int32)

    def front(index):
        return init[pl.ds(pl.multiple_of(index * piece, piece), piece), :]

    for copy in copies:
        copy.wait()
    near_ref[...] = front(core * fronts + z)
    last_ref[...] = front((core + 1 + xh + xl) % 2 * fronts + z)
    sent_ref[rows:rows + piece, :] = front((1 - core) * fronts + z)
    for part, image in enumerate(half_image(init, sent_ref, orbits, core == 1, block)):
        put(sent_ref, part, image, orbits, order)


def kept_kernel(orbits, order, block, init_ref, sent_ref, own_ref):
    core = lax.axis_index("core")
    for part, image in enumerate(half_image(init_ref, sent_ref, orbits, core == 0, block)):
        put(own_ref, part, image, orbits, order)


def second_kernel(orbits, order, block, front_ref, sent_ref, got_ref, out_ref):
    core = lax.axis_index("core")
    half_rows = front_ref.shape[0] // 2

    def part_of(part):
        halves = [
            front_ref[pl.ds(half * half_rows + part, half_rows // 2, stride=2), :]
            for half in range(2)
        ]
        return jnp.where(core == 0, halves[0], halves[1]), jnp.where(core == 0, halves[1], halves[0])

    left_re, left_im = [], []
    for re, im in zip(part_of(0), part_of(1)):
        sigma_re, sigma_im = sigma_pair(re, im, orbits)
        left_re += [sigma_re, re]
        left_im += [sigma_im, im]
    images = image_of(
        jnp.concatenate(left_re, axis=1), jnp.concatenate(left_im, axis=1),
        (sent_ref, got_ref), block)
    lanes = out_ref.shape[1]
    straight = (core + 1 + lax.axis_index("xh")) % 2 == 0
    for part, image in enumerate(images):
        low, high = image[:, :lanes], image[:, lanes:]
        first, second = jnp.where(straight, low, high), jnp.where(straight, high, low)
        put(out_ref, part, jnp.concatenate([first, second], axis=1), orbits, order)


VMEM = pl.BlockSpec(memory_space=pltpu.VMEM)
LIMIT = pltpu.CompilerParams(vmem_limit_bytes=12 << 20)


def first_collide(init, green, field, orbits, order):
    rows, width = init.shape
    operands = [pltpu.with_memory_space_constraint(x, pltpu.HBM) for x in (init, green, field)]
    return pl.pallas_call(
        functools.partial(first_kernel, orbits, order),
        out_shape=[
            jax.ShapeDtypeStruct((n, width), kind) for n, kind in (
                (rows + 2 * orbits + 2 * green.shape[0], jnp.float32), (2 * orbits, jnp.float32),
                (2 * orbits, jnp.float32), (8, jnp.int32), (rows, jnp.float32))
        ],
        in_specs=[pl.BlockSpec(memory_space=pltpu.HBM)] * 3,
        out_specs=[VMEM] * 5,
        scratch_shapes=[pltpu.SemaphoreType.DMA((3,))],
        compiler_params=LIMIT,
        name="first_collide",
    )(*operands)


def kept_collide(init, sent, orbits, order, block):
    return pl.pallas_call(
        functools.partial(kept_kernel, orbits, order, block),
        out_shape=jax.ShapeDtypeStruct(init.shape, jnp.float32),
        in_specs=[VMEM] * 2,
        out_specs=VMEM,
        compiler_params=LIMIT,
        cost_estimate=pl.CostEstimate(flops=10**8, bytes_accessed=10**6, transcendentals=0),
        name="kept_collide",
    )(init, sent)


def second_collide(front, histories, orbits, order, block):
    return pl.pallas_call(
        functools.partial(second_kernel, orbits, order, block),
        out_shape=jax.ShapeDtypeStruct(front.shape, jnp.float32),
        in_specs=[VMEM] * 3,
        out_specs=VMEM,
        compiler_params=LIMIT,
        name="second_collide",
    )(front, *histories)


def per_device(turns, ys, zs, front_init, green_hist, field_hist):
    return corrector(turns, ys, zs, front_init, green_hist, field_hist)


def corrector(turns, ys, zs, front_init, green_hist, field_hist):
    fronts, orbits, parts, width = front_init.shape
    rows = fronts * orbits * parts
    init = front_init.reshape(rows, width)

    def tiles(history):
        times, inner, _, lanes = history.shape
        return history.reshape(times, inner, parts, lanes // width, width).transpose(
            0, 1, 3, 2, 4).reshape(-1, width)

    def swap(value):
        return lax.ppermute(value, "core", [(0, 1), (1, 0)])

    def reduced(partial_sum):
        spread = lax.all_to_all(partial_sum.reshape(fronts, -1, width), A, 0, 0, tiled=True)
        return jnp.sum(spread, axis=0)

    def gathered(copies):
        return lax.all_to_all(copies, B, 0, 0, tiled=True).reshape(rows, width)

    def copies_of(start, turned):
        piece = start + STEP_WEIGHT * turned
        return jnp.broadcast_to(piece[None], (fronts,) + piece.shape)

    green, field = tiles(green_hist), tiles(field_hist)
    order = [(y + zs // 2) % zs for y in range(ys)]
    block = green.shape[0]
    sent, near, last, flag, init = first_collide(init, green, field, orbits, order)
    got = swap(sent)
    own = kept_collide(init, sent, orbits, order, block)
    flag = jnp.broadcast_to(flag == 0, (2, rows // 16, 8, width))
    own, flag = lax.optimization_barrier((own, flag))
    piece = reduced(own + got[:rows])
    near = jnp.where(
        lax.axis_index("xh") == lax.axis_index("core"), near, got[rows:rows + 2 * orbits])
    current = gathered(copies_of(near, lax.ppermute(piece, EVERY, turns[0])))
    image = second_collide(current, (sent, got), orbits, order, block)
    turned = lax.ppermute(reduced(image), EVERY, turns[1])
    final = gathered(copies_of(last, turned)).reshape(2, -1, 8, width)
    return jnp.where(flag, final, final[::-1]).reshape(front_init.shape)


def solution(mesh):
    xls, ys, cores, xhs, zs = 2, 8, 2, 2, 8
    fine = Mesh(mesh.devices.reshape(xls, ys, cores, xhs, zs), EVERY)

    def place(xl, y, core, xh, z):
        return (((xl * ys + y) * cores + core) * xhs + xh) * zs + z

    everyone = [
        (xl, y, core, xh, z)
        for xl in range(xls) for y in range(ys) for core in range(cores)
        for xh in range(xhs) for z in range(zs)
    ]
    turns = [
        [(place(xl, y, core, xh, z), place(xh, z, core, xl, (y + zs // 2) % zs))
         for xl, y, core, xh, z in everyone],
        [(place(xl, y, core, xh, z), place(xh, z, core if xl != xh else 1 - core, xl, (y + zs // 2) % zs))
         for xl, y, core, xh, z in everyone],
    ]
    return jax.shard_map(
        functools.partial(per_device, turns, ys, zs),
        mesh=fine,
        in_specs=(
            P(None, None, None, ("xl", "y", "core")),
            P(("xl", "y", "core"), None, None, B),
            P(("xl", "y", "core"), None, None, B),
        ),
        out_specs=P(None, None, None, ("xl", "y", "core")),
        check_vma=False,
    )
```

```python
import functools

import jax
import jax.numpy as jnp
from jax import lax
from jax.experimental import pallas as pl
from jax.experimental.pallas import tpu as pltpu
from jax.sharding import Mesh, PartitionSpec as P


STEP_WEIGHT = 0.5

A = ("xl", "y")
B = ("xh", "z")
EVERY = ("xl", "y", "core", "xh", "z")


def split(value):
    high = value.astype(jnp.bfloat16)
    low = (value - high.astype(jnp.float32)).astype(jnp.bfloat16)
    return high, low


def swap_orbitals(value, orbits):
    rows, lanes = value.shape
    row = lax.broadcasted_iota(jnp.int32, value.shape, 0)
    lane = lax.broadcasted_iota(jnp.int32, value.shape, 1)
    step = 1
    while step < orbits:
        row_bit = (row // step) % 2
        lane_bit = (lane // step) % 2
        up = pltpu.roll(pltpu.roll(value, step, 1), rows - step, 0)
        down = pltpu.roll(pltpu.roll(value, lanes - step, 1), step, 0)
        value = jnp.where(row_bit == lane_bit, value, jnp.where(row_bit == 0, up, down))
        step *= 2
    return value


def sigma_pair(re, im, orbits):
    other_re = swap_orbitals(re, orbits)
    other_im = swap_orbitals(im, orbits)
    square_re = re * re - im * im
    square_im = 2.0 * re * im
    return (
        square_re * other_re + square_im * other_im,
        square_im * other_re - square_re * other_im,
    )


def history(refs, part, block):
    depth = block // 4
    halves = [
        jnp.concatenate([
            ref[pl.ds(ref.shape[0] - last * block + 2 * half + part, depth, stride=4), :]
            for ref in refs for last in (2, 1)
        ], axis=0)
        for half in range(2)
    ]
    return jnp.concatenate(halves, axis=1)


def image_of(left_re, left_im, refs, block):
    (re_high, re_low), (im_high, im_low) = split(left_re), split(left_im)
    right_re, right_im = split(history(refs, 0, block)), split(history(refs, 1, block))

    def one(re_first, im_first, first, second):
        left = jnp.concatenate(
            [re_first[0], im_first[0], re_first[0], im_first[0], re_first[1], im_first[1]], axis=1)
        right = jnp.concatenate(
            [first[0], second[0], first[1], second[1], first[0], second[0]], axis=0)
        return jnp.dot(left, right, preferred_element_type=jnp.float32)

    re, im = (re_high, re_low), (im_high, im_low)
    return one(re, (-im_high, -im_low), right_re, right_im), one(re, im, right_im, right_re)


def put(target_ref, part, image, orbits, order):
    lanes = target_ref.shape[1]
    for half in range(2):
        for place, front in enumerate(order):
            first = (half * len(order) + place) * 2 * orbits + part
            target_ref[pl.ds(first, orbits, stride=2), :] = image[
                front * orbits:(front + 1) * orbits, half * lanes:(half + 1) * lanes]


def half_image(front_ref, buffer_ref, orbits, block):
    pairs = orbits * orbits // 2
    re, im = (front_ref[pl.ds(part, pairs, stride=2), :] for part in range(2))
    sigma_re, sigma_im = sigma_pair(re, im, orbits)
    return image_of(
        jnp.concatenate([sigma_re, re], axis=1), jnp.concatenate([sigma_im, im], axis=1),
        (buffer_ref,), block)


def load_kernel(fronts, init_ref, green_ref, field_ref,
                sent_ref, mine_ref, last_ref, flag_ref, sems):
    core, xl, xh, z = (lax.axis_index(axis) for axis in ("core", "xl", "xh", "z"))
    half, piece, block = mine_ref.shape[0], last_ref.shape[0], green_ref.shape[0]

    def rows_of(index, count):
        return init_ref.at[pl.ds(pl.multiple_of(index * count, count), count)]

    copies = [
        pltpu.make_async_copy(source, target, sems.at[n])
        for n, (source, target) in enumerate((
            (rows_of(1 - core, half), sent_ref.at[pl.ds(0, half)]),
            (green_ref, sent_ref.at[pl.ds(half, block)]),
            (field_ref, sent_ref.at[pl.ds(half + block, block)]),
            (rows_of(core, half), mine_ref),
            (rows_of((core + 1 + xh + xl) % 2 * fronts + z, piece), last_ref),
        ))
    ]
    for copy in copies:
        copy.start()
    flag_ref[...] = jnp.full(flag_ref.shape, (core + 1 + xl) % 2, jnp.int32)
    for copy in copies:
        copy.wait()


def near_kernel(orbits, order, block, mine_ref, sent_ref, own_ref):
    for part, image in enumerate(half_image(mine_ref, sent_ref, orbits, block)):
        put(own_ref, part, image, orbits, order)


def far_kernel(orbits, order, block, mine_ref, own_ref, got_ref, chip_ref, piece_ref):
    core, xh, z = (lax.axis_index(axis) for axis in ("core", "xh", "z"))
    piece = piece_ref.shape[0]
    here = pl.ds(pl.multiple_of(z * piece, piece), piece)
    piece_ref[...] = jnp.where(xh == core, mine_ref[here, :], got_ref[here, :])
    for part, image in enumerate(half_image(got_ref, got_ref, orbits, block)):
        put(chip_ref, part, image, orbits, order)
    chip_ref[...] += own_ref[...]


def second_kernel(orbits, order, block, front_ref, sent_ref, got_ref, out_ref):
    core = lax.axis_index("core")
    half_rows = front_ref.shape[0] // 2

    def part_of(part):
        halves = [
            front_ref[pl.ds(half * half_rows + part, half_rows // 2, stride=2), :]
            for half in range(2)
        ]
        return jnp.where(core == 0, halves[0], halves[1]), jnp.where(core == 0, halves[1], halves[0])

    left_re, left_im = [], []
    for re, im in zip(part_of(0), part_of(1)):
        sigma_re, sigma_im = sigma_pair(re, im, orbits)
        left_re += [sigma_re, re]
        left_im += [sigma_im, im]
    images = image_of(
        jnp.concatenate(left_re, axis=1), jnp.concatenate(left_im, axis=1),
        (sent_ref, got_ref), block)
    lanes = out_ref.shape[1]
    straight = (core + 1 + lax.axis_index("xh")) % 2 == 0
    for part, image in enumerate(images):
        low, high = image[:, :lanes], image[:, lanes:]
        first, second = jnp.where(straight, low, high), jnp.where(straight, high, low)
        put(out_ref, part, jnp.concatenate([first, second], axis=1), orbits, order)


VMEM = pl.BlockSpec(memory_space=pltpu.VMEM)
LIMIT = pltpu.CompilerParams(vmem_limit_bytes=12 << 20)


def load(init, green, field, fronts):
    rows, width = init.shape
    operands = [pltpu.with_memory_space_constraint(x, pltpu.HBM) for x in (init, green, field)]
    return pl.pallas_call(
        functools.partial(load_kernel, fronts // 2),
        out_shape=[
            jax.ShapeDtypeStruct((n, width), kind) for n, kind in (
                (rows // 2 + 2 * green.shape[0], jnp.float32), (rows // 2, jnp.float32),
                (rows // fronts, jnp.float32), (8, jnp.int32))
        ],
        in_specs=[pl.BlockSpec(memory_space=pltpu.HBM)] * 3,
        out_specs=[VMEM] * 4,
        scratch_shapes=[pltpu.SemaphoreType.DMA((5,))],
        compiler_params=LIMIT,
        name="load",
    )(*operands)


def near_collide(mine, sent, orbits, order, block):
    rows, width = mine.shape
    return pl.pallas_call(
        functools.partial(near_kernel, orbits, order, block),
        out_shape=jax.ShapeDtypeStruct((2 * rows, width), jnp.float32),
        in_specs=[VMEM] * 2,
        out_specs=VMEM,
        compiler_params=LIMIT,
        cost_estimate=pl.CostEstimate(flops=10**8, bytes_accessed=10**6, transcendentals=0),
        name="near_collide",
    )(mine, sent)


def far_collide(mine, own, got, orbits, order, block):
    return pl.pallas_call(
        functools.partial(far_kernel, orbits, order, block),
        out_shape=[
            jax.ShapeDtypeStruct((n, own.shape[1]), jnp.float32)
            for n in (own.shape[0], 2 * orbits)
        ],
        in_specs=[VMEM] * 3,
        out_specs=[VMEM] * 2,
        compiler_params=LIMIT,
        name="far_collide",
    )(mine, own, got)


def second_collide(front, histories, orbits, order, block):
    return pl.pallas_call(
        functools.partial(second_kernel, orbits, order, block),
        out_shape=jax.ShapeDtypeStruct(front.shape, jnp.float32),
        in_specs=[VMEM] * 3,
        out_specs=VMEM,
        compiler_params=LIMIT,
        name="second_collide",
    )(front, *histories)


def per_device(turns, ys, zs, front_init, green_hist, field_hist):
    return corrector(turns, ys, zs, front_init, green_hist, field_hist)


def corrector(turns, ys, zs, front_init, green_hist, field_hist):
    fronts, orbits, parts, width = front_init.shape
    rows = fronts * orbits * parts
    init = front_init.reshape(rows, width)

    def tiles(history):
        times, inner, _, lanes = history.shape
        return history.reshape(times, inner, parts, lanes // width, width).transpose(
            0, 1, 3, 2, 4).reshape(-1, width)

    def swap(value):
        return lax.ppermute(value, "core", [(0, 1), (1, 0)])

    def reduced(partial_sum):
        spread = lax.all_to_all(partial_sum.reshape(fronts, -1, width), A, 0, 0, tiled=True)
        return jnp.sum(spread, axis=0)

    def gathered(copies):
        return lax.all_to_all(copies, B, 0, 0, tiled=True).reshape(rows, width)

    def copies_of(start, turned):
        piece = start + STEP_WEIGHT * turned
        return jnp.broadcast_to(piece[None], (fronts,) + piece.shape)

    green, field = tiles(green_hist), tiles(field_hist)
    order = [(y + zs // 2) % zs for y in range(ys)]
    block = green.shape[0]
    sent, mine, last, flag = load(init, green, field, fronts)
    got = swap(sent)
    own = near_collide(mine, sent, orbits, order, block)
    flag = jnp.broadcast_to(flag == 0, (2, rows // 16, 8, width))
    own, flag = lax.optimization_barrier((own, flag))
    chip, near = far_collide(mine, own, got, orbits, order, block)
    current = gathered(copies_of(near, lax.ppermute(reduced(chip), EVERY, turns[0])))
    image = second_collide(current, (sent, got), orbits, order, block)
    turned = lax.ppermute(reduced(image), EVERY, turns[1])
    final = gathered(copies_of(last, turned)).reshape(2, -1, 8, width)
    return jnp.where(flag, final, final[::-1]).reshape(front_init.shape)


def solution(mesh):
    xls, ys, cores, xhs, zs = 2, 8, 2, 2, 8
    fine = Mesh(mesh.devices.reshape(xls, ys, cores, xhs, zs), EVERY)

    def place(xl, y, core, xh, z):
        return (((xl * ys + y) * cores + core) * xhs + xh) * zs + z

    everyone = [
        (xl, y, core, xh, z)
        for xl in range(xls) for y in range(ys) for core in range(cores)
        for xh in range(xhs) for z in range(zs)
    ]
    turns = [
        [(place(xl, y, core, xh, z), place(xh, z, core, xl, (y + zs // 2) % zs))
         for xl, y, core, xh, z in everyone],
        [(place(xl, y, core, xh, z), place(xh, z, core if xl != xh else 1 - core, xl, (y + zs // 2) % zs))
         for xl, y, core, xh, z in everyone],
    ]
    return jax.shard_map(
        functools.partial(per_device, turns, ys, zs),
        mesh=fine,
        in_specs=(
            P(None, None, None, ("xl", "y", "core")),
            P(("xl", "y", "core"), None, None, B),
            P(("xl", "y", "core"), None, None, B),
        ),
        out_specs=P(None, None, None, ("xl", "y", "core")),
        check_vma=False,
    )
```

```python
import functools

import jax
import jax.numpy as jnp
from jax import lax
from jax.experimental import pallas as pl
from jax.experimental.pallas import tpu as pltpu
from jax.sharding import Mesh, PartitionSpec as P


STEP_WEIGHT = 0.5

A = ("xl", "y")
B = ("xh", "z")
EVERY = ("xl", "y", "core", "xh", "z")


def split(value):
    high = value.astype(jnp.bfloat16)
    low = (value - high.astype(jnp.float32)).astype(jnp.bfloat16)
    return high, low


def swap_orbitals(value, orbits):
    rows, lanes = value.shape
    row = lax.broadcasted_iota(jnp.int32, value.shape, 0)
    lane = lax.broadcasted_iota(jnp.int32, value.shape, 1)
    step = 1
    while step < orbits:
        row_bit = (row // step) % 2
        lane_bit = (lane // step) % 2
        up = pltpu.roll(pltpu.roll(value, step, 1), rows - step, 0)
        down = pltpu.roll(pltpu.roll(value, lanes - step, 1), step, 0)
        value = jnp.where(row_bit == lane_bit, value, jnp.where(row_bit == 0, up, down))
        step *= 2
    return value


def sigma_pair(re, im, orbits):
    other_re = swap_orbitals(re, orbits)
    other_im = swap_orbitals(im, orbits)
    square_re = re * re - im * im
    square_im = 2.0 * re * im
    return (
        square_re * other_re + square_im * other_im,
        square_im * other_re - square_re * other_im,
    )


def history(refs, part, block):
    depth = block // 4
    halves = [
        jnp.concatenate([
            ref[pl.ds(ref.shape[0] - last * block + 2 * half + part, depth, stride=4), :]
            for ref in refs for last in (2, 1)
        ], axis=0)
        for half in range(2)
    ]
    return jnp.concatenate(halves, axis=1)


def image_of(left_re, left_im, refs, block):
    (re_high, re_low), (im_high, im_low) = split(left_re), split(left_im)
    right_re, right_im = split(history(refs, 0, block)), split(history(refs, 1, block))

    def one(re_first, im_first, first, second):
        left = jnp.concatenate(
            [re_first[0], im_first[0], re_first[0], im_first[0], re_first[1], im_first[1]], axis=1)
        right = jnp.concatenate(
            [first[0], second[0], first[1], second[1], first[0], second[0]], axis=0)
        return jnp.dot(left, right, preferred_element_type=jnp.float32)

    re, im = (re_high, re_low), (im_high, im_low)
    return one(re, (-im_high, -im_low), right_re, right_im), one(re, im, right_im, right_re)


def put(target_ref, part, image, orbits, order, base_ref=None):
    lanes = target_ref.shape[1]
    for half in range(2):
        for place, front in enumerate(order):
            first = (half * len(order) + place) * 2 * orbits + part
            here = pl.ds(first, orbits, stride=2)
            value = image[front * orbits:(front + 1) * orbits, half * lanes:(half + 1) * lanes]
            target_ref[here, :] = value if base_ref is None else value + base_ref[here, :]


def half_image(front_ref, buffer_ref, orbits, block):
    pairs = orbits * orbits // 2
    re, im = (front_ref[pl.ds(part, pairs, stride=2), :] for part in range(2))
    sigma_re, sigma_im = sigma_pair(re, im, orbits)
    return image_of(
        jnp.concatenate([sigma_re, re], axis=1), jnp.concatenate([sigma_im, im], axis=1),
        (buffer_ref,), block)


def load_kernel(fronts, init_ref, green_ref, field_ref,
                sent_ref, mine_ref, last_ref, flag_ref, sems):
    core, xl, xh, z = (lax.axis_index(axis) for axis in ("core", "xl", "xh", "z"))
    half, piece, block = mine_ref.shape[0], last_ref.shape[0], green_ref.shape[0]

    def rows_of(index, count):
        return init_ref.at[pl.ds(pl.multiple_of(index * count, count), count)]

    copies = [
        pltpu.make_async_copy(source, target, sems.at[n])
        for n, (source, target) in enumerate((
            (rows_of(1 - core, half), sent_ref.at[pl.ds(0, half)]),
            (green_ref, sent_ref.at[pl.ds(half, block)]),
            (field_ref, sent_ref.at[pl.ds(half + block, block)]),
            (rows_of(core, half), mine_ref),
            (rows_of((core + 1 + xh + xl) % 2 * fronts + z, piece), last_ref),
        ))
    ]
    for copy in copies:
        copy.start()
    flag_ref[...] = jnp.full(flag_ref.shape, (core + 1 + xl) % 2, jnp.int32)
    for copy in copies:
        copy.wait()


def near_kernel(orbits, order, block, mine_ref, sent_ref, own_ref):
    for part, image in enumerate(half_image(mine_ref, sent_ref, orbits, block)):
        put(own_ref, part, image, orbits, order)


def far_kernel(orbits, order, block, mine_ref, own_ref, got_ref, chip_ref, piece_ref):
    core, xh, z = (lax.axis_index(axis) for axis in ("core", "xh", "z"))
    piece = piece_ref.shape[0]
    here = pl.ds(pl.multiple_of(z * piece, piece), piece)
    piece_ref[...] = jnp.where(xh == core, mine_ref[here, :], got_ref[here, :])
    for part, image in enumerate(half_image(got_ref, got_ref, orbits, block)):
        put(chip_ref, part, image, orbits, order, own_ref)


def second_kernel(orbits, order, block, front_ref, sent_ref, got_ref, out_ref):
    core = lax.axis_index("core")
    half_rows = front_ref.shape[0] // 2

    def part_of(part):
        halves = [
            front_ref[pl.ds(half * half_rows + part, half_rows // 2, stride=2), :]
            for half in range(2)
        ]
        return jnp.where(core == 0, halves[0], halves[1]), jnp.where(core == 0, halves[1], halves[0])

    left_re, left_im = [], []
    for re, im in zip(part_of(0), part_of(1)):
        sigma_re, sigma_im = sigma_pair(re, im, orbits)
        left_re += [sigma_re, re]
        left_im += [sigma_im, im]
    images = image_of(
        jnp.concatenate(left_re, axis=1), jnp.concatenate(left_im, axis=1),
        (sent_ref, got_ref), block)
    lanes = out_ref.shape[1]
    straight = (core + 1 + lax.axis_index("xh")) % 2 == 0
    for part, image in enumerate(images):
        low, high = image[:, :lanes], image[:, lanes:]
        first, second = jnp.where(straight, low, high), jnp.where(straight, high, low)
        put(out_ref, part, jnp.concatenate([first, second], axis=1), orbits, order)


VMEM = pl.BlockSpec(memory_space=pltpu.VMEM)
LIMIT = pltpu.CompilerParams(vmem_limit_bytes=12 << 20)


def load(init, green, field, fronts):
    rows, width = init.shape
    operands = [pltpu.with_memory_space_constraint(x, pltpu.HBM) for x in (init, green, field)]
    return pl.pallas_call(
        functools.partial(load_kernel, fronts // 2),
        out_shape=[
            jax.ShapeDtypeStruct((n, width), kind) for n, kind in (
                (rows // 2 + 2 * green.shape[0], jnp.float32), (rows // 2, jnp.float32),
                (rows // fronts, jnp.float32), (8, jnp.int32))
        ],
        in_specs=[pl.BlockSpec(memory_space=pltpu.HBM)] * 3,
        out_specs=[VMEM] * 4,
        scratch_shapes=[pltpu.SemaphoreType.DMA((5,))],
        compiler_params=LIMIT,
        name="load",
    )(*operands)


def near_collide(mine, sent, orbits, order, block):
    rows, width = mine.shape
    return pl.pallas_call(
        functools.partial(near_kernel, orbits, order, block),
        out_shape=jax.ShapeDtypeStruct((2 * rows, width), jnp.float32),
        in_specs=[VMEM] * 2,
        out_specs=VMEM,
        compiler_params=LIMIT,
        cost_estimate=pl.CostEstimate(flops=10**8, bytes_accessed=10**6, transcendentals=0),
        name="near_collide",
    )(mine, sent)


def far_collide(mine, own, got, orbits, order, block):
    return pl.pallas_call(
        functools.partial(far_kernel, orbits, order, block),
        out_shape=[
            jax.ShapeDtypeStruct((n, own.shape[1]), jnp.float32)
            for n in (own.shape[0], 2 * orbits)
        ],
        in_specs=[VMEM] * 3,
        out_specs=[VMEM] * 2,
        compiler_params=LIMIT,
        name="far_collide",
    )(mine, own, got)


def second_collide(front, histories, orbits, order, block):
    return pl.pallas_call(
        functools.partial(second_kernel, orbits, order, block),
        out_shape=jax.ShapeDtypeStruct(front.shape, jnp.float32),
        in_specs=[VMEM] * 3,
        out_specs=VMEM,
        compiler_params=LIMIT,
        name="second_collide",
    )(front, *histories)


def per_device(turns, ys, zs, front_init, green_hist, field_hist):
    return corrector(turns, ys, zs, front_init, green_hist, field_hist)


def corrector(turns, ys, zs, front_init, green_hist, field_hist):
    fronts, orbits, parts, width = front_init.shape
    rows = fronts * orbits * parts
    init = front_init.reshape(rows, width)

    def tiles(history):
        times, inner, _, lanes = history.shape
        return history.reshape(times, inner, parts, lanes // width, width).transpose(
            0, 1, 3, 2, 4).reshape(-1, width)

    def swap(value):
        return lax.ppermute(value, "core", [(0, 1), (1, 0)])

    def reduced(partial_sum):
        spread = lax.all_to_all(partial_sum.reshape(fronts, -1, width), A, 0, 0, tiled=True)
        return jnp.sum(spread, axis=0)

    def gathered(copies):
        return lax.all_to_all(copies, B, 0, 0, tiled=True).reshape(rows, width)

    def copies_of(start, turned):
        piece = start + STEP_WEIGHT * turned
        return jnp.broadcast_to(piece[None], (fronts,) + piece.shape)

    green, field = tiles(green_hist), tiles(field_hist)
    order = [(y + zs // 2) % zs for y in range(ys)]
    block = green.shape[0]
    sent, mine, last, flag = load(init, green, field, fronts)
    got = swap(sent)
    own = near_collide(mine, sent, orbits, order, block)
    flag = jnp.broadcast_to(flag == 0, (2, rows // 16, 8, width))
    own, flag = lax.optimization_barrier((own, flag))
    chip, near = far_collide(mine, own, got, orbits, order, block)
    current = gathered(copies_of(near, lax.ppermute(reduced(chip), EVERY, turns[0])))
    image = second_collide(current, (sent, got), orbits, order, block)
    turned = lax.ppermute(reduced(image), EVERY, turns[1])
    final = gathered(copies_of(last, turned)).reshape(2, -1, 8, width)
    return jnp.where(flag, final, final[::-1]).reshape(front_init.shape)


def solution(mesh):
    xls, ys, cores, xhs, zs = 2, 8, 2, 2, 8
    fine = Mesh(mesh.devices.reshape(xls, ys, cores, xhs, zs), EVERY)

    def place(xl, y, core, xh, z):
        return (((xl * ys + y) * cores + core) * xhs + xh) * zs + z

    everyone = [
        (xl, y, core, xh, z)
        for xl in range(xls) for y in range(ys) for core in range(cores)
        for xh in range(xhs) for z in range(zs)
    ]
    turns = [
        [(place(xl, y, core, xh, z), place(xh, z, core, xl, (y + zs // 2) % zs))
         for xl, y, core, xh, z in everyone],
        [(place(xl, y, core, xh, z), place(xh, z, core if xl != xh else 1 - core, xl, (y + zs // 2) % zs))
         for xl, y, core, xh, z in everyone],
    ]
    return jax.shard_map(
        functools.partial(per_device, turns, ys, zs),
        mesh=fine,
        in_specs=(
            P(None, None, None, ("xl", "y", "core")),
            P(("xl", "y", "core"), None, None, B),
            P(("xl", "y", "core"), None, None, B),
        ),
        out_specs=P(None, None, None, ("xl", "y", "core")),
        check_vma=False,
    )
```

```python
import functools

import jax
import jax.numpy as jnp
from jax import lax
from jax.experimental import pallas as pl
from jax.experimental.pallas import tpu as pltpu
from jax.sharding import Mesh, PartitionSpec as P


STEP_WEIGHT = 0.5

A = ("xl", "y")
B = ("xh", "z")
EVERY = ("xl", "y", "core", "xh", "z")


def split(value):
    high = value.astype(jnp.bfloat16)
    low = (value - high.astype(jnp.float32)).astype(jnp.bfloat16)
    return high, low


def swap_orbitals(value, orbits):
    rows, lanes = value.shape
    row = lax.broadcasted_iota(jnp.int32, value.shape, 0)
    lane = lax.broadcasted_iota(jnp.int32, value.shape, 1)
    step = 1
    while step < orbits:
        row_bit = (row // step) % 2
        lane_bit = (lane // step) % 2
        up = pltpu.roll(pltpu.roll(value, step, 1), rows - step, 0)
        down = pltpu.roll(pltpu.roll(value, lanes - step, 1), step, 0)
        value = jnp.where(row_bit == lane_bit, value, jnp.where(row_bit == 0, up, down))
        step *= 2
    return value


def sigma_pair(re, im, orbits):
    other_re = swap_orbitals(re, orbits)
    other_im = swap_orbitals(im, orbits)
    square_re = re * re - im * im
    square_im = 2.0 * re * im
    return (
        square_re * other_re + square_im * other_im,
        square_im * other_re - square_re * other_im,
    )


def history(refs, part, block):
    depth = block // 4
    halves = [
        jnp.concatenate([
            ref[pl.ds(ref.shape[0] - last * block + 2 * half + part, depth, stride=4), :]
            for ref in refs for last in (2, 1)
        ], axis=0)
        for half in range(2)
    ]
    return jnp.concatenate(halves, axis=1)


def image_of(left_re, left_im, refs, block):
    (re_high, re_low), (im_high, im_low) = split(left_re), split(left_im)
    right_re, right_im = split(history(refs, 0, block)), split(history(refs, 1, block))

    def one(re_first, im_first, first, second):
        left = jnp.concatenate(
            [re_first[0], im_first[0], re_first[0], im_first[0], re_first[1], im_first[1]], axis=1)
        right = jnp.concatenate(
            [first[0], second[0], first[1], second[1], first[0], second[0]], axis=0)
        return jnp.dot(left, right, preferred_element_type=jnp.float32)

    re, im = (re_high, re_low), (im_high, im_low)
    return one(re, (-im_high, -im_low), right_re, right_im), one(re, im, right_im, right_re)


def put(target_ref, part, image, orbits, order):
    lanes = target_ref.shape[1]
    for half in range(2):
        for place, front in enumerate(order):
            first = (half * len(order) + place) * 2 * orbits + part
            target_ref[pl.ds(first, orbits, stride=2), :] = image[
                front * orbits:(front + 1) * orbits, half * lanes:(half + 1) * lanes]


def half_image(front_ref, buffer_ref, orbits, block):
    pairs = orbits * orbits // 2
    re, im = (front_ref[pl.ds(part, pairs, stride=2), :] for part in range(2))
    sigma_re, sigma_im = sigma_pair(re, im, orbits)
    return image_of(
        jnp.concatenate([sigma_re, re], axis=1), jnp.concatenate([sigma_im, im], axis=1),
        (buffer_ref,), block)


def load_kernel(init_ref, green_ref, field_ref,
                sent_ref, flag_ref, sems):
    core, xl = lax.axis_index("core"), lax.axis_index("xl")
    half, block = init_ref.shape[0] // 2, green_ref.shape[0]

    def rows_of(index, count):
        return init_ref.at[pl.ds(pl.multiple_of(index * count, count), count)]

    copies = [
        pltpu.make_async_copy(source, target, sems.at[n])
        for n, (source, target) in enumerate((
            (rows_of(1 - core, half), sent_ref.at[pl.ds(0, half)]),
            (green_ref, sent_ref.at[pl.ds(half, block)]),
            (field_ref, sent_ref.at[pl.ds(half + block, block)]),
        ))
    ]
    for copy in copies:
        copy.start()
    flag_ref[...] = jnp.full(flag_ref.shape, (core + 1 + xl) % 2, jnp.int32)
    for copy in copies:
        copy.wait()


def near_kernel(orbits, order, block, init_ref, sent_ref, own_ref, mine_ref, last_ref, sems):
    core, xl, xh, z = (lax.axis_index(axis) for axis in ("core", "xl", "xh", "z"))
    half, piece = mine_ref.shape[0], last_ref.shape[0]
    last = ((core + 1 + xh + xl) % 2 * len(order) + z) * piece
    copies = [
        pltpu.make_async_copy(
            init_ref.at[pl.ds(pl.multiple_of(start, count), count)], target, sems.at[n])
        for n, (start, count, target) in enumerate(
            ((core * half, half, mine_ref), (last, piece, last_ref)))
    ]
    for copy in copies:
        copy.start()
    for copy in copies:
        copy.wait()
    for part, image in enumerate(half_image(mine_ref, sent_ref, orbits, block)):
        put(own_ref, part, image, orbits, order)


def far_kernel(orbits, order, block, mine_ref, own_ref, got_ref, chip_ref, piece_ref):
    core, xh, z = (lax.axis_index(axis) for axis in ("core", "xh", "z"))
    piece = piece_ref.shape[0]
    here = pl.ds(pl.multiple_of(z * piece, piece), piece)
    piece_ref[...] = jnp.where(xh == core, mine_ref[here, :], got_ref[here, :])
    for part, image in enumerate(half_image(got_ref, got_ref, orbits, block)):
        put(chip_ref, part, image, orbits, order)
    chip_ref[...] += own_ref[...]


def second_kernel(orbits, order, block, front_ref, sent_ref, got_ref, out_ref):
    core = lax.axis_index("core")
    half_rows = front_ref.shape[0] // 2

    def part_of(part):
        halves = [
            front_ref[pl.ds(half * half_rows + part, half_rows // 2, stride=2), :]
            for half in range(2)
        ]
        return jnp.where(core == 0, halves[0], halves[1]), jnp.where(core == 0, halves[1], halves[0])

    left_re, left_im = [], []
    for re, im in zip(part_of(0), part_of(1)):
        sigma_re, sigma_im = sigma_pair(re, im, orbits)
        left_re += [sigma_re, re]
        left_im += [sigma_im, im]
    images = image_of(
        jnp.concatenate(left_re, axis=1), jnp.concatenate(left_im, axis=1),
        (sent_ref, got_ref), block)
    lanes = out_ref.shape[1]
    straight = (core + 1 + lax.axis_index("xh")) % 2 == 0
    for part, image in enumerate(images):
        low, high = image[:, :lanes], image[:, lanes:]
        first, second = jnp.where(straight, low, high), jnp.where(straight, high, low)
        put(out_ref, part, jnp.concatenate([first, second], axis=1), orbits, order)


VMEM = pl.BlockSpec(memory_space=pltpu.VMEM)
LIMIT = pltpu.CompilerParams(vmem_limit_bytes=12 << 20)


def load(init, green, field):
    rows, width = init.shape
    operands = [pltpu.with_memory_space_constraint(x, pltpu.HBM) for x in (init, green, field)]
    return pl.pallas_call(
        load_kernel,
        out_shape=[
            jax.ShapeDtypeStruct((n, width), kind) for n, kind in (
                (rows // 2 + 2 * green.shape[0], jnp.float32), (8, jnp.int32))
        ],
        in_specs=[pl.BlockSpec(memory_space=pltpu.HBM)] * 3,
        out_specs=[VMEM] * 2,
        scratch_shapes=[pltpu.SemaphoreType.DMA((3,))],
        compiler_params=LIMIT,
        name="load",
    )(*operands)


def near_collide(init, sent, orbits, order, block):
    rows, width = init.shape
    init = pltpu.with_memory_space_constraint(init, pltpu.HBM)
    return pl.pallas_call(
        functools.partial(near_kernel, orbits, order, block),
        out_shape=[
            jax.ShapeDtypeStruct((n, width), jnp.float32) for n in (rows, rows // 2, 2 * orbits)
        ],
        in_specs=[pl.BlockSpec(memory_space=pltpu.HBM), VMEM],
        out_specs=[VMEM] * 3,
        scratch_shapes=[pltpu.SemaphoreType.DMA((2,))],
        compiler_params=LIMIT,
        cost_estimate=pl.CostEstimate(flops=10**8, bytes_accessed=10**6, transcendentals=0),
        name="near_collide",
    )(init, sent)


def far_collide(mine, own, got, orbits, order, block):
    return pl.pallas_call(
        functools.partial(far_kernel, orbits, order, block),
        out_shape=[
            jax.ShapeDtypeStruct((n, own.shape[1]), jnp.float32)
            for n in (own.shape[0], 2 * orbits)
        ],
        in_specs=[VMEM] * 3,
        out_specs=[VMEM] * 2,
        compiler_params=LIMIT,
        name="far_collide",
    )(mine, own, got)


def second_collide(front, histories, orbits, order, block):
    return pl.pallas_call(
        functools.partial(second_kernel, orbits, order, block),
        out_shape=jax.ShapeDtypeStruct(front.shape, jnp.float32),
        in_specs=[VMEM] * 3,
        out_specs=VMEM,
        compiler_params=LIMIT,
        name="second_collide",
    )(front, *histories)


def per_device(turns, ys, zs, front_init, green_hist, field_hist):
    return corrector(turns, ys, zs, front_init, green_hist, field_hist)


def corrector(turns, ys, zs, front_init, green_hist, field_hist):
    fronts, orbits, parts, width = front_init.shape
    rows = fronts * orbits * parts
    init = front_init.reshape(rows, width)

    def tiles(history):
        times, inner, _, lanes = history.shape
        return history.reshape(times, inner, parts, lanes // width, width).transpose(
            0, 1, 3, 2, 4).reshape(-1, width)

    def swap(value):
        return lax.ppermute(value, "core", [(0, 1), (1, 0)])

    def reduced(partial_sum):
        spread = lax.all_to_all(partial_sum.reshape(fronts, -1, width), A, 0, 0, tiled=True)
        return jnp.sum(spread, axis=0)

    def gathered(copies):
        return lax.all_to_all(copies, B, 0, 0, tiled=True).reshape(rows, width)

    def copies_of(start, turned):
        piece = start + STEP_WEIGHT * turned
        return jnp.broadcast_to(piece[None], (fronts,) + piece.shape)

    green, field = tiles(green_hist), tiles(field_hist)
    order = [(y + zs // 2) % zs for y in range(ys)]
    block = green.shape[0]
    sent, flag = load(init, green, field)
    got = swap(sent)
    own, mine, last = near_collide(init, sent, orbits, order, block)
    flag = jnp.broadcast_to(flag == 0, (2, rows // 16, 8, width))
    own, flag = lax.optimization_barrier((own, flag))
    chip, near = far_collide(mine, own, got, orbits, order, block)
    current = gathered(copies_of(near, lax.ppermute(reduced(chip), EVERY, turns[0])))
    image = second_collide(current, (sent, got), orbits, order, block)
    turned = lax.ppermute(reduced(image), EVERY, turns[1])
    final = gathered(copies_of(last, turned)).reshape(2, -1, 8, width)
    return jnp.where(flag, final, final[::-1]).reshape(front_init.shape)


def solution(mesh):
    xls, ys, cores, xhs, zs = 2, 8, 2, 2, 8
    fine = Mesh(mesh.devices.reshape(xls, ys, cores, xhs, zs), EVERY)

    def place(xl, y, core, xh, z):
        return (((xl * ys + y) * cores + core) * xhs + xh) * zs + z

    everyone = [
        (xl, y, core, xh, z)
        for xl in range(xls) for y in range(ys) for core in range(cores)
        for xh in range(xhs) for z in range(zs)
    ]
    turns = [
        [(place(xl, y, core, xh, z), place(xh, z, core, xl, (y + zs // 2) % zs))
         for xl, y, core, xh, z in everyone],
        [(place(xl, y, core, xh, z), place(xh, z, core if xl != xh else 1 - core, xl, (y + zs // 2) % zs))
         for xl, y, core, xh, z in everyone],
    ]
    return jax.shard_map(
        functools.partial(per_device, turns, ys, zs),
        mesh=fine,
        in_specs=(
            P(None, None, None, ("xl", "y", "core")),
            P(("xl", "y", "core"), None, None, B),
            P(("xl", "y", "core"), None, None, B),
        ),
        out_specs=P(None, None, None, ("xl", "y", "core")),
        check_vma=False,
    )
```
